32 devices in a mesh: sub: 16 (over z, y, x), grp: 2 (over core).
Axes of the slice: x: 2, y: 2, z: 4, core: 2. Of those that a mesh axis runs over, the one named last changes fastest.
Arguments:
- interior_factor: bfloat16 [16, 1024, 1024], P('sub'), may hold values from -2 to 2, as said below
- coupling: bfloat16 [16, 512, 1024], P('sub', 'grp'), may hold values from -0.09375 to 0.09375
- boundary_stiffness: float32 [16, 512, 512], P('sub', 'grp'), may hold values from -0.65625 to 9, as said below
- interior_mass: float32 [16, 1024], P('sub'), may hold values from 0.5 to 4
- boundary_mass: float32 [16, 512], P('sub', 'grp'), may hold values from 0.5 to 2
- dof_map: int32 [16, 256], P('sub'), may hold values from 0 to 255, each once within a row
- load_cases: float32 [16, 64, 256], P('sub'), may hold values from -30 to 30
Outputs:
- reduced_stiffness: float32 [16, 256, 256], P('sub')
- reduced_mass: float32 [16, 256, 256], P('sub')
- displacement: float32 [16, 64, 256], P('sub')
The draws below stay inside these ranges and needn't reach their ends.
Inputs may be any that keep to these rules, and one draw needn't show every extreme that they name: `interior_factor`: lower triangular; diagonal between 1 and 2. `boundary_stiffness`: symmetric; diagonal between 6 and 9. `dof_map`: each row a permutation of 0 to 255.
All inputs are finite; a program needn't handle non-finite values.
Results may differ from the reference program's by a relative error of at most 0.00095.
Values may be sent and summed in bfloat16 or wider, within the bound.
A program may use at most 64 MiB of HBM per device.

```python
import math
import jax
import jax.numpy as jnp
from jax import lax

NI = 1024
NB = 512
NRHS = 64
ITERS = 2
FACE = 256
NS = 16


def draw_interior_factor(key, part):
    first_key, second_key = jax.random.split(jax.random.fold_in(key, 11))
    lower_part = jnp.clip(jax.random.normal(first_key, (NS, NI, NI), jnp.float32), -4.0, 4.0) * (1.0 / NI ** 0.5)
    diagonal = jax.random.uniform(second_key, (NS, NI), jnp.float32, 1.0, 2.0)
    lower_part = jnp.tril(lower_part, -1)
    result = lower_part + jnp.eye(NI, dtype=jnp.float32)[None] * diagonal[:, None, :]
    return result.astype(jnp.bfloat16)


def draw_coupling(key, part):
    first_key = jax.random.fold_in(jax.random.fold_in(key, 37), 0)
    entries = jnp.clip(jax.random.normal(first_key, (NS, NB, NI), jnp.float32), -4.0, 4.0)
    result = entries * (0.5 / NI ** 0.5)
    return result.astype(jnp.bfloat16)


def draw_boundary_stiffness(key, part):
    first_key, second_key = jax.random.split(jax.random.fold_in(key, 23))
    raw = jnp.clip(jax.random.normal(first_key, (NS, NB, NB), jnp.float32), -4.0, 4.0)
    diagonal = jax.random.uniform(second_key, (NS, NB), jnp.float32, 6.0, 9.0)
    symmetric = (raw + jnp.swapaxes(raw, 1, 2)) / (2.0 * NB) ** 0.5
    row_face = lax_rows = jnp.arange(NB, dtype=jnp.int32)[:, None] < NB // 2
    col_face = jnp.arange(NB, dtype=jnp.int32)[None, :] < NB // 2
    same_face = row_face == col_face
    profile = jnp.where(same_face, 0.3, 2.6).astype(jnp.float32)
    eye_mask = jnp.eye(NB, dtype=jnp.float32)[None]
    return symmetric * profile[None] * (1.0 - eye_mask) + eye_mask * diagonal[:, None, :]


def block_levels(own_key, dims, cuts, smallest, largest):
    def one(axis_at, shards_of):
        steps = jax.random.uniform(jax.random.fold_in(jax.random.fold_in(own_key, 6), axis_at), (shards_of,), jnp.float32, smallest / len(cuts), largest / len(cuts))
        return jnp.repeat(jnp.exp(steps), dims[axis_at] // shards_of).reshape((-1,) + (1,) * (len(dims) - axis_at - 1))

    factor_of = one(*cuts[0])
    for cut in cuts[1:]:
        factor_of = factor_of * one(*cut)
    return factor_of


def normal_values(stream_key, shape, spread, bound, cuts=(), held_as=jnp.bfloat16):
    drawn = spread * jax.random.normal(stream_key, shape, jnp.float32)
    if cuts:
        drawn = drawn * block_levels(stream_key, shape, cuts, -0.22, 0.18)
    return jnp.clip(drawn, -bound, bound).astype(held_as)


def setup_inputs(seed: int = 0) -> dict:
    key_list = jax.random.split(jax.random.key(seed), 8)
    return {
        "interior_factor": draw_interior_factor(jax.random.fold_in(key_list[7], 71), 0),
        "coupling": draw_coupling(jax.random.fold_in(key_list[7], 71), 0),
        "boundary_stiffness": draw_boundary_stiffness(jax.random.fold_in(key_list[7], 71), 0),
        "interior_mass": jnp.clip(jnp.exp(math.log(4.0) - 2.0794415 * jax.random.uniform(key_list[3], (NS, NI), jnp.float32) ** block_levels(key_list[3], (NS, NI), ((0, 16),), -0.2, 0.2)), 0.5, 4.0),
        "boundary_mass": jnp.clip(jnp.exp(math.log(2.0) - 1.3862944 * jax.random.uniform(key_list[4], (NS, NB), jnp.float32) ** block_levels(key_list[4], (NS, NB), ((0, 16), (1, 2)), -0.2, 0.2)), 0.5, 2.0),
        "dof_map": jax.vmap(lambda own: jax.random.permutation(own, FACE))(jax.random.split(key_list[5], NS)).reshape((NS, FACE)).astype(jnp.int32),
        "load_cases": normal_values(key_list[6], (NS, NRHS, FACE), 5.0, 30.0, ((0, 16),), jnp.float32),
    }


HIGH = lax.Precision.HIGHEST

def reduce_single(items):
    factor_low, coupling_rows, stiff, weights, bound_mass = items
    factor = factor_low.astype(jnp.float32)
    modes_w = jax.scipy.linalg.solve_triangular(factor, coupling_rows.astype(jnp.float32).T, lower=True)
    constraint = -jax.scipy.linalg.solve_triangular(factor, modes_w, lower=True, trans=1)
    schur = stiff - jnp.dot(modes_w.T, modes_w, precision=HIGH)
    mass_red = jnp.diag(bound_mass) + jnp.dot(constraint.T, weights[:, None] * constraint, precision=HIGH)
    return (schur, mass_red)

def invert_map(mapping):
    count = mapping.shape[0]
    return jnp.zeros((count,), jnp.int32).at[mapping].set(jnp.arange(count, dtype=jnp.int32))

def reference(interior_factor, coupling, boundary_stiffness, interior_mass, boundary_mass, dof_map, load_cases):
    schur_all, mass_all = lax.map(reduce_single, (interior_factor, coupling, boundary_stiffness, interior_mass, boundary_mass))
    half = FACE
    inverse = jax.vmap(invert_map)(dof_map)
    permute = jax.vmap(lambda block, order: block[order][:, order])
    shared_stiff = permute(schur_all[:, half:, half:], inverse)
    shared_mass = permute(mass_all[:, half:, half:], inverse)
    reduced_stiffness = schur_all[:, :half, :half] + jnp.roll(shared_stiff, -1, axis=0)
    reduced_mass = mass_all[:, :half, :half] + jnp.roll(shared_mass, -1, axis=0)
    factors = jax.vmap(jnp.linalg.cholesky)(reduced_stiffness)

    def precondition(values):
        return jax.vmap(lambda low, rows: jax.scipy.linalg.cho_solve((low, True), rows.T).T)(factors, values)

    def operate(values):
        previous = jnp.roll(values, 1, axis=0)
        taken = jax.vmap(lambda rows, order: jnp.take(rows, order, axis=1))(previous, dof_map)
        local_dirs = jnp.concatenate([values, taken], axis=2)
        images = jnp.einsum('snb,scb->snc', local_dirs, schur_all, precision=HIGH)
        owned = images[:, :, :half]
        shared = jax.vmap(lambda rows, order: jnp.take(rows, order, axis=1))(images[:, :, half:], inverse)
        return owned + jnp.roll(shared, -1, axis=0)

    def inner_sum(left, right):
        return jnp.einsum('snf,smf->nm', left, right, precision=HIGH)

    def chol_solve(matrix, right):
        return jax.scipy.linalg.cho_solve((jnp.linalg.cholesky(matrix), True), right)
    solution = jnp.zeros_like(load_cases)
    residual = load_cases
    smoothed = precondition(residual)
    rho_sum = inner_sum(residual, smoothed)
    direction = smoothed
    for step in range(ITERS):
        images = operate(direction)
        gamma_sum = inner_sum(direction, images)
        step_coeffs = chol_solve(gamma_sum, rho_sum)
        solution = solution + jnp.einsum('mn,smf->snf', step_coeffs, direction, precision=HIGH)
        residual = residual - jnp.einsum('mn,smf->snf', step_coeffs, images, precision=HIGH)
        if step + 1 < ITERS:
            smoothed = precondition(residual)
            rho_next = inner_sum(residual, smoothed)
            next_coeffs = chol_solve(rho_sum, rho_next)
            direction = smoothed + jnp.einsum('mn,smf->snf', next_coeffs, direction, precision=HIGH)
            rho_sum = rho_next
    return (reduced_stiffness, reduced_mass, solution)
```

```python
import functools
import jax
import jax.numpy as jnp
from jax import lax
from jax.experimental import pallas as pl
from jax.experimental.pallas import tpu as pltpu
from jax.sharding import PartitionSpec as P

F32 = jnp.float32
BF16 = jnp.bfloat16
HIGH = lax.Precision.HIGHEST
SMALL = 128
TILE = 256
VMEM_LIMIT = 56 * 2**20
NT = (((1,), (1,)), ((), ()))
NN = (((1,), (0,)), ((), ()))
TN = (((0,), (0,)), ((), ()))


def dot(a, b, dims=NN):
    return lax.dot_general(a, b, dims, preferred_element_type=F32)


def fdot(a, b, dims=NN):
    return lax.dot_general(a, b, dims, precision=HIGH, preferred_element_type=F32)


def split(x):
    hi = x.astype(BF16)
    return hi, (x - hi.astype(F32)).astype(BF16)


def dot3(a, b, dims=NN):
    ah, al = split(a)
    bh, bl = split(b)
    return dot(ah, bh, dims) + (dot(ah, bl, dims) + dot(al, bh, dims))


def iota(shape, dim):
    return lax.broadcasted_iota(jnp.int32, shape, dim)


def invert_diagonal(l_ref, inv, small, between):
    count = l_ref.shape[0] // SMALL
    rows = iota((SMALL, SMALL), 0)
    cols = iota((SMALL, SMALL), 1)

    def block(j):
        return l_ref[j * SMALL : (j + 1) * SMALL, j * SMALL : (j + 1) * SMALL]

    pair = ((rows >> 1) == (cols >> 1)) & (rows > cols)
    for j in range(count):
        full = block(j).astype(F32)
        diag = jnp.where(rows == cols, full, 0.0)
        down = 1.0 / jnp.sum(diag, axis=1, keepdims=True)
        across = 1.0 / jnp.sum(diag, axis=0, keepdims=True)
        first = jnp.where(rows == cols, down, 0.0)
        small[j] = first - jnp.where(pair, down * full * across, 0.0)

    def level(lev, carry):
        same = (rows >> (lev + 1)) == (cols >> (lev + 1))
        low = ((rows >> lev) & 1) > ((cols >> lev) & 1)
        mask = same & low
        for j in range(count):
            x = small[j]
            off = jnp.where(mask, block(j).astype(F32), 0.0).astype(BF16)
            xh, xl = split(x)
            mid = dot(jnp.concatenate([xh, xl], 1), jnp.concatenate([off, off], 0))
            mh, ml = split(mid)
            wide = dot(jnp.concatenate([mh, ml], 1), jnp.concatenate([xh, xh], 0))
            small[j] = x - (wide + dot(mh, xl))
        return carry

    lax.fori_loop(1, 3, level, 0)
    between()
    lax.fori_loop(3, SMALL.bit_length() - 1, level, 0)
    for j in range(count // 2):
        upper, lower = small[2 * j], small[2 * j + 1]
        off = l_ref[(2 * j + 1) * SMALL : (2 * j + 2) * SMALL, 2 * j * SMALL : (2 * j + 1) * SMALL]
        lh, ll = split(lower)
        mid = dot(jnp.concatenate([lh, ll], 1), jnp.concatenate([off, off], 0))
        inv[j, :SMALL, :SMALL] = upper
        inv[j, :SMALL, SMALL:] = jnp.zeros((SMALL, SMALL), F32)
        inv[j, SMALL:, :SMALL] = -dot3(mid, upper)
        inv[j, SMALL:, SMALL:] = lower


def solve_modes(l_ref, c_ref, inv, wh, wl):
    for j in range(l_ref.shape[0] // TILE):
        at = slice(j * TILE, (j + 1) * TILE)
        acc = c_ref[:, at].astype(F32)
        if j:
            before = slice(0, j * TILE)
            acc = acc - (
                dot(wh[:, before], l_ref[at, before], NT)
                + dot(wl[:, before], l_ref[at, before], NT)
            )
        wh[:, at], wl[:, at] = split(dot3(acc, inv[j], NT))


def solve_constraint(l_ref, inv, wh, wl):
    ni = l_ref.shape[0]
    for j in reversed(range(ni // TILE)):
        at = slice(j * TILE, (j + 1) * TILE)
        acc = wh[:, at].astype(F32) + wl[:, at].astype(F32)
        if (j + 1) * TILE < ni:
            after = slice((j + 1) * TILE, ni)
            acc = acc + (dot(wh[:, after], l_ref[after, at]) + dot(wl[:, after], l_ref[after, at]))
        wh[:, at], wl[:, at] = split(-dot3(acc, inv[j]))


def inverse_of(p):
    m = len(p)
    if m == 1:
        return [[1.0 / p[0][0]]]
    if m == 2:
        scale = 1.0 / (p[0][0] * p[1][1] - p[0][1] * p[0][1])
        side = -p[0][1] * scale
        return [[p[1][1] * scale, side], [side, p[0][0] * scale]]
    h = m // 2
    span = range(h)
    ai = inverse_of([row[:h] for row in p[:h]])
    b = [row[h:] for row in p[:h]]
    w = [[sum(ai[i][k] * b[k][j] for k in span) for j in span] for i in span]
    s = [[None] * h for _ in span]
    for i in span:
        for j in range(i, h):
            s[i][j] = s[j][i] = p[h + i][h + j] - sum(b[k][i] * w[k][j] for k in span)
    si = inverse_of(s)
    v = [[sum(w[i][k] * si[k][j] for k in span) for j in span] for i in span]
    top = [[None] * h for _ in span]
    for i in span:
        for j in range(i, h):
            top[i][j] = top[j][i] = ai[i][j] + sum(v[i][k] * w[j][k] for k in span)
    out = [top[i] + [-v[i][j] for j in span] for i in span]
    return out + [[-v[j][i] for j in span] + si[i] for i in span]


def sweep(a, size, pivots=8):
    width = a.shape[1]
    lane = iota(a.shape, 1)
    row_at = iota(a.shape, 0)
    first = lane < size
    local = jnp.where(first, lane, lane - size)
    local_row = local[:1]

    def lanes(rows, k):
        left = rows[:, k : k + 1]
        if width == size:
            return jnp.broadcast_to(left, rows.shape)
        return jnp.where(first[: rows.shape[0]], left, rows[:, size + k : size + k + 1])

    for k in range(0, size, pivots):
        span = range(pivots)
        cols = [lanes(a, k + i) for i in span]
        rows = [a[k + i : k + i + 1, :] for i in span]
        small = [[cols[j][k + i : k + i + 1] for j in span] for i in span]
        small = [[small[min(i, j)][max(i, j)] for j in span] for i in span]
        inv = inverse_of(small)
        fresh = []
        for i in span:
            row = sum(inv[i][j] * rows[j] for j in span)
            for j in span:
                row = jnp.where(local_row == k + j, inv[i][j], row)
            fresh.append(row)
        inside = (local // pivots) == (k // pivots)
        a = jnp.where(inside, 0.0, a)
        for i in span:
            a = a - cols[i] * fresh[i]
        for i in span:
            a = jnp.where(row_at == k + i, fresh[i], a)
    return a


def invert(ref, step):
    n = ref.shape[0]
    for p in range(n // step):
        at = slice(p * step, (p + 1) * step)
        pin = sweep(ref[at, at], step)
        panel = ref[at, :]
        col = ref[:, at]
        inside = (iota((step, n), 1) // step) == p
        row = jnp.where(inside, 0.0, dot3(pin, panel))
        left = (iota((n, step), 0) // step) == p
        colz = jnp.where(left, 0.0, col)
        ref[...] = ref[...] - dot3(colz, row)
        ref[:, at] = -dot3(colz, pin)
        ref[at, :] = row
        ref[at, at] = pin


STEP = 64


def stages_of(size):
    stages, stride = [], 1
    while stride < size:
        radix = 4 if stride * 4 <= size else 2
        stages.append((stride, radix))
        stride *= radix
    return stages


def at_device(sub, grp):
    return dict(device_id=(sub, grp), device_id_type=pl.DeviceIdType.MESH)


def pick(q, x):
    hi, lo = split(x)
    rest = (x - hi.astype(F32) - lo.astype(F32)).astype(BF16)
    return dot(q, hi) + dot(q, lo) + dot(q, rest)


def pick_columns(x, q):
    hi, lo = split(x)
    rest = (x - hi.astype(F32) - lo.astype(F32)).astype(BF16)
    return dot(hi, q, NT) + dot(lo, q, NT) + dot(rest, q, NT)


def reduction_kernel(
    l_hbm, c_hbm, rows_hbm, weights_hbm, bound_hbm, map_hbm, loads_hbm,
    red_ref, mass_ref, out_ref,
    l_ref, c_ref, weights_ref, bound, map_ref, loads_ref, stiff,
    inv, small, wh, wl, move, came,
    work, z, step, near, acc, got, total, acc_last, got_last,
    local, send, recv, part_send, part_recv, fwd_send, fwd_recv,
    dir_send, dir_recv, sum_send, sum_recv, all_send, all_recv, last_send, last_recv,
):
    grp, sub = lax.axis_index("grp"), lax.axis_index("sub")
    members, size = lax.axis_size("grp"), lax.axis_size("sub")
    ahead, back = lax.rem(sub + 1, size), lax.rem(sub + size - 1, size)
    others = [lax.rem(grp + d, members) for d in range(1, members)]
    width = c_hbm.shape[0]
    half = map_ref.shape[1]
    n = loads_ref.shape[0]
    tiles = l_ref.shape[0] // TILE
    stages = stages_of(size)
    mine = pl.ds(pl.multiple_of(grp * width, width), width)
    share = half // members
    part = pl.ds(pl.multiple_of(grp * share, share), share)

    loads_in = []

    def load(src, dst):
        copy = pltpu.make_async_copy(src, dst, local.at[len(loads_in)])
        copy.start()
        loads_in.append(copy)

    spans = [slice(j * TILE, (j + 1) * TILE) for j in range(tiles)]
    for at in spans:
        load(l_hbm.at[at, at], l_ref.at[at, at])
    load(map_hbm, map_ref)
    load(c_hbm, c_ref.at[mine])
    load(rows_hbm, stiff.at[mine])
    load(bound_hbm, bound.at[grp])
    for j in range(1, tiles):
        before = slice(0, j * TILE)
        load(l_hbm.at[spans[j], before], l_ref.at[spans[j], before])
    load(weights_hbm, weights_ref)
    load(loads_hbm, loads_ref)

    def partner(stride, radix, d):
        digit = lax.rem(lax.div(sub, stride), radix)
        return sub + (lax.rem(digit + d, radix) - digit) * stride

    barrier = pltpu.get_barrier_semaphore()
    greeted = 0
    for other in others:
        pl.semaphore_signal(barrier, inc=1, **at_device(sub, other))
        greeted += 1
    for to in [ahead, back] + [partner(t, r, d) for t, r in stages for d in range(1, r)]:
        pl.semaphore_signal(barrier, inc=1, **at_device(to, grp))
        greeted += 1

    def remote(src, dst, send, recv, to_sub, to_grp):
        copy = pltpu.make_async_remote_copy(
            src_ref=src, dst_ref=dst, send_sem=send, recv_sem=recv, **at_device(to_sub, to_grp)
        )
        copy.start()
        return copy

    def spread(item, src, dst):
        return [
            remote(src, dst, send.at[item, d], recv.at[item, d], sub, other)
            for d, other in enumerate(others)
        ]

    def to_back(item, ref):
        return remote(ref.at[part], came.at[item, part], part_send.at[item], part_recv.at[item], back, grp)

    def forward(item):
        return [
            remote(
                came.at[item, part], came.at[item, part],
                fwd_send.at[item, d], fwd_recv.at[item, d], sub, other,
            )
            for d, other in enumerate(others)
        ]

    def finished(copies):
        for copy in copies:
            copy.wait()

    shared_in = []

    def exchange():
        finished(loads_in[tiles:])
        pl.semaphore_wait(barrier, greeted)
        shared_in.extend(spread(0, c_ref.at[mine], c_ref.at[mine]))
        shared_in.extend(spread(1, stiff.at[mine], stiff.at[mine]))
        shared_in.extend(spread(2, bound.at[grp], bound.at[grp]))

    finished(loads_in[:tiles])
    invert_diagonal(l_ref, inv, small, exchange)
    finished(shared_in)

    q = jnp.where(iota((half, half), 0) == map_ref[...], 1.0, 0.0)
    qb = q.astype(BF16)
    c_ref[half:, :] = dot(qb, c_ref[half:, :]).astype(BF16)
    stiff[half:, :] = pick(qb, stiff[half:, :])
    stiff[half:, half:] = pick_columns(stiff[half:, half:], qb)
    solve_modes(l_ref, c_ref, inv, wh, wl)
    wo, ws = wh[:half, :], wh[half:, :]
    move[0] = stiff[half:, half:] - dot(ws, ws, NT)
    stiff_move = to_back(0, move.at[0])
    move[1] = stiff[half:, :half] - dot(ws, wo, NT)
    cross_move = to_back(1, move.at[1])
    work[...] = stiff[:half, :half] - dot(wo, wo, NT)

    solve_constraint(l_ref, inv, wh, wl)
    stiff_move.wait()
    forwards = forward(0)
    weights = weights_ref[...]
    eye = iota((half, half), 0) == iota((half, half), 1)
    pieces = jnp.concatenate([bound[i] for i in range(members)], axis=1)

    def mass_of(c, b):
        ch, cl = split(c.astype(F32) * weights)
        return dot(ch, c, NT) + dot(cl, c, NT) + jnp.where(eye, b, 0.0)

    placed = jnp.sum(q * pieces[:, half:], axis=1, keepdims=True)
    move[2] = mass_of(wh[half:, :], placed)
    mass_move = to_back(2, move.at[2])
    finished(forwards)
    reduced = work[...] + came[0]
    red_ref[...] = reduced
    work[...] = reduced
    cross_move.wait()
    cross_forwards = forward(1)
    invert(work, STEP)

    z[...] = dot3(loads_ref[...], work[...])
    copies = [
        remote(z, near.at[0], dir_send.at[0], dir_recv.at[0], ahead, grp),
        remote(z, near.at[1], dir_send.at[1], dir_recv.at[1], back, grp),
    ]
    acc[0, :n, :n] = fdot(loads_ref[...], z[...], NT)
    acc[0, n:, n:] = jnp.zeros((n, n), F32)
    mass_ref[...] = mass_of(wh[:half, :], pieces[:, :half])
    mass_move.wait()
    mass_forwards = forward(2)
    finished(cross_forwards)
    finished(copies)
    pull = dot3(near[0], move[1]) + dot3(near[1], came[1], NT)
    step[...] = dot3(pull, work[...])
    copies = [remote(step, near.at[2], dir_send.at[2], dir_recv.at[2], ahead, grp)]
    acc[0, :n, n:] = fdot(z[...], pull, NT)
    acc[0, n:, :n] = fdot(pull, step[...], NT)

    rows = 2 * n // members
    chunk = pl.ds(pl.multiple_of(grp * rows, rows), rows)
    slots = [sum(r - 1 for _, r in stages[:i]) for i in range(len(stages))]

    def send_sums(i):
        stride, radix = stages[i]
        return [
            remote(
                acc.at[i, chunk], got.at[slots[i] + d - 1],
                sum_send.at[slots[i] + d - 1], sum_recv.at[slots[i] + d - 1],
                partner(stride, radix, d), grp,
            )
            for d in range(1, radix)
        ]

    def add_sums(i, copies):
        value = acc[i, chunk, :]
        for d, copy in enumerate(copies):
            copy.wait()
            value = value + got[slots[i] + d]
        acc[i + 1, chunk, :] = value

    def send_last(i):
        stride, radix = stages[i]
        return [
            remote(
                acc_last.at[i], got_last.at[slots[i] + d - 1],
                last_send.at[slots[i] + d - 1], last_recv.at[slots[i] + d - 1],
                partner(stride, radix, d), grp,
            )
            for d in range(1, radix)
        ]

    def add_last(i, copies):
        value = acc_last[i]
        for d, copy in enumerate(copies):
            copy.wait()
            value = value + got_last[slots[i] + d]
        acc_last[i + 1] = value

    final = len(stages)
    sums = send_sums(0)
    finished(mass_forwards)
    mass_ref[...] = mass_ref[...] + came[2]
    for i in range(1, final):
        add_sums(i - 1, sums)
        sums = send_sums(i)
    finished(copies)
    taken = dot3(near[2], move[1])
    acc_last[0] = fdot(step[...], taken, NT) + fdot(taken, step[...], NT)
    lasts = send_last(0)
    add_sums(final - 1, sums)
    total[chunk, :] = acc[final, chunk, :]
    copies = [
        remote(acc.at[final, chunk], total.at[chunk], all_send.at[d], all_recv.at[d], sub, other)
        for d, other in enumerate(others)
    ]
    for i in range(1, final):
        add_last(i - 1, lasts)
        lasts = send_last(i)
    finished(copies)

    rho, side = total[:n, :n], total[:n, n:]
    bend = total[n:, :n]
    gamma, kappa = rho + side, side + bend
    gamma_inv = sweep(gamma, n)
    base = fdot(gamma_inv, rho)
    lift = fdot(gamma_inv, kappa)
    fixed = bend - fdot(kappa, lift)
    right = side - fdot(lift, rho, TN)
    add_last(final - 1, lasts)
    second = fdot(sweep(fixed + acc_last[final], n), right)
    out_ref[...] = fdot(base - fdot(lift, second), z[...], TN) + fdot(second, step[...], TN)


def hand_over(*refs):
    count = len(refs) // 2
    for src, dst in zip(refs[:count], refs[count:]):
        dst[...] = src[...]


def shards(
    interior_factor, coupling, boundary_stiffness, interior_mass, boundary_mass, dof_map, load_cases
):
    width, ni = coupling.shape[1:]
    nbound = boundary_stiffness.shape[2]
    half = nbound // 2
    n = load_cases.shape[1]
    size, members = lax.axis_size("sub"), lax.axis_size("grp")
    block = jax.ShapeDtypeStruct((half, half), F32)
    shapes = [block, block, jax.ShapeDtypeStruct((n, half), F32)]
    stages = stages_of(size)
    slots = sum(r - 1 for _, r in stages)
    peers = max(members - 1, 1)
    dma = pltpu.SemaphoreType.DMA
    vmem = pl.BlockSpec(memory_space=pltpu.VMEM)
    outs = pl.pallas_call(
        reduction_kernel,
        out_shape=shapes,
        in_specs=[pl.BlockSpec(memory_space=pltpu.HBM)] * 7,
        out_specs=[vmem] * 3,
        scratch_shapes=[
            pltpu.VMEM((ni, ni), BF16),
            pltpu.VMEM((nbound, ni), BF16),
            pltpu.VMEM((1, ni), F32),
            pltpu.VMEM((members, 1, width), F32),
            pltpu.VMEM((1, half), jnp.int32),
            pltpu.VMEM((n, half), F32),
            pltpu.VMEM((nbound, nbound), F32),
            pltpu.VMEM((ni // TILE, TILE, TILE), F32),
            pltpu.VMEM((ni // SMALL, SMALL, SMALL), F32),
            pltpu.VMEM((nbound, ni), BF16),
            pltpu.VMEM((nbound, ni), BF16),
            pltpu.VMEM((3, half, half), F32),
            pltpu.VMEM((3, half, half), F32),
            pltpu.VMEM((half, half), F32),
            pltpu.VMEM((n, half), F32),
            pltpu.VMEM((n, half), F32),
            pltpu.VMEM((3, n, half), F32),
            pltpu.VMEM((len(stages) + 1, 2 * n, 2 * n), F32),
            pltpu.VMEM((slots, 2 * n // members, 2 * n), F32),
            pltpu.VMEM((2 * n, 2 * n), F32),
            pltpu.VMEM((len(stages) + 1, n, n), F32),
            pltpu.VMEM((slots, n, n), F32),
            dma((2 * (ni // TILE) + 5,)),
            dma((3, peers)), dma((3, peers)), dma((3,)), dma((3,)), dma((3, peers)), dma((3, peers)),
            dma((3,)), dma((3,)), dma((slots,)), dma((slots,)), dma((peers,)), dma((peers,)),
            dma((slots,)), dma((slots,)),
        ],
        compiler_params=pltpu.CompilerParams(
            vmem_limit_bytes=VMEM_LIMIT, collective_id=0, has_side_effects=True
        ),
        name="reduction",
    )(
        interior_factor[0], coupling[0], boundary_stiffness[0], interior_mass,
        boundary_mass, dof_map, load_cases[0],
    )
    outs = pl.pallas_call(
        hand_over, out_shape=shapes, in_specs=[vmem] * 3, out_specs=[vmem] * 3, name="hand_over"
    )(*outs)
    return tuple(out[None] for out in outs)


def solution(mesh):
    return jax.shard_map(
        shards,
        mesh=mesh,
        in_specs=(
            P("sub", None, None),
            P("sub", "grp", None),
            P("sub", "grp", None),
            P("sub", None),
            P("sub", "grp"),
            P("sub", None),
            P("sub", None, None),
        ),
        out_specs=(P("sub", None, None), P("sub", None, None), P("sub", None, None)),
        check_vma=False,
    )
```

```python
import functools
import jax
import jax.numpy as jnp
from jax import lax
from jax.experimental import pallas as pl
from jax.experimental.pallas import tpu as pltpu
from jax.sharding import PartitionSpec as P

F32 = jnp.float32
BF16 = jnp.bfloat16
HIGH = lax.Precision.HIGHEST
SMALL = 128
BASE = 32
TILE = 256
VMEM_LIMIT = 56 * 2**20
NT = (((1,), (1,)), ((), ()))
NN = (((1,), (0,)), ((), ()))
TN = (((0,), (0,)), ((), ()))


def dot(a, b, dims=NN):
    return lax.dot_general(a, b, dims, preferred_element_type=F32)


def fdot(a, b, dims=NN):
    return lax.dot_general(a, b, dims, precision=HIGH, preferred_element_type=F32)


def split(x):
    hi = x.astype(BF16)
    return hi, (x - hi.astype(F32)).astype(BF16)


def dot3(a, b, dims=NN):
    ah, al = split(a)
    bh, bl = split(b)
    return dot(ah, bh, dims) + (dot(ah, bl, dims) + dot(al, bh, dims))


def iota(shape, dim):
    return lax.broadcasted_iota(jnp.int32, shape, dim)


def pickers_of(pickers):
    base = pickers.shape[0]
    rows = iota((SMALL, 2 * SMALL), 0)
    lane = iota((1, 2 * SMALL), 1)
    start = (lane & (SMALL - BASE)) + (lane >> SMALL.bit_length() - 1)
    for k in range(base):
        pickers[k] = jnp.where(rows == start + 2 * k, 1.0, 0.0).astype(BF16)


def invert_diagonal(l_ref, inv, pickers, strips, between):
    count = l_ref.shape[0] // SMALL
    rows = iota((SMALL, SMALL), 0)
    cols = iota((SMALL, SMALL), 1)
    bands = range(SMALL // BASE)

    def block(j):
        return l_ref[j * SMALL : (j + 1) * SMALL, j * SMALL : (j + 1) * SMALL]

    band = iota((BASE, SMALL), 1) >> BASE.bit_length() - 1
    for j in range(count):
        full = block(j).astype(F32)
        strips[j * BASE : (j + 1) * BASE, :] = sum(
            jnp.where(band == b, full[b * BASE : (b + 1) * BASE], 0.0) for b in bands
        )
    packed = jnp.concatenate(
        [strips[pl.ds(i, count, stride=BASE), :] for i in range(BASE)], axis=0
    ).astype(BF16)
    spread = [dot(packed[2 * k * count :], pickers[k]) for k in range(BASE // 2)]

    def entry(i, k):
        at = (i - (k & -2)) * count
        side = (k & 1) * SMALL
        return spread[k >> 1][at : at + count, side : side + SMALL]

    place = iota((count, SMALL), 1) & (BASE - 1)
    done = [jnp.where(place == i, 1.0, 0.0) for i in range(BASE)]
    scale = [1.0 / entry(i, i) for i in range(BASE)]
    for k in range(BASE):
        done[k] = done[k] * scale[k]
        for i in range(k + 1, BASE):
            done[i] = done[i] - entry(i, k) * done[k]
    for i in range(BASE):
        strips[pl.ds(i, count, stride=BASE), :] = done[i]
    between()

    xs = []
    for j in range(count):
        strip = strips[j * BASE : (j + 1) * BASE, :]
        xs.append(jnp.concatenate([jnp.where(band == b, strip, 0.0) for b in bands], axis=0))
    size = BASE
    while size < SMALL:
        same = (rows // (2 * size)) == (cols // (2 * size))
        mask = same & ((rows & size) > (cols & size))
        pairs = range(SMALL // (2 * size))
        for j in range(count):
            x = xs[j]
            parts = [x[p * size : (p + 1) * size] for p in range(2 * len(pairs))]
            low = jnp.concatenate(parts[1::2], axis=0)
            off = jnp.where(mask, block(j).astype(F32), 0.0).astype(BF16)
            lh, ll = split(low)
            xh, xl = split(x)
            mid = dot(jnp.concatenate([lh, ll], 1), jnp.concatenate([off, off], 0))
            mh, ml = split(mid)
            wide = dot(jnp.concatenate([mh, ml], 1), jnp.concatenate([xh, xh], 0)) + dot(mh, xl)
            low = low - wide
            for p in pairs:
                parts[2 * p + 1] = low[p * size : (p + 1) * size]
            xs[j] = jnp.concatenate(parts, axis=0)
        size *= 2

    for j in range(count // 2):
        upper, lower = xs[2 * j], xs[2 * j + 1]
        off = l_ref[(2 * j + 1) * SMALL : (2 * j + 2) * SMALL, 2 * j * SMALL : (2 * j + 1) * SMALL]
        lh, ll = split(lower)
        mid = dot(jnp.concatenate([lh, ll], 1), jnp.concatenate([off, off], 0))
        inv[j, :SMALL, :SMALL] = upper
        inv[j, :SMALL, SMALL:] = jnp.zeros((SMALL, SMALL), F32)
        inv[j, SMALL:, :SMALL] = -dot3(mid, upper)
        inv[j, SMALL:, SMALL:] = lower


def solve_modes(l_ref, c_ref, inv, wh, wl):
    for j in range(l_ref.shape[0] // TILE):
        at = slice(j * TILE, (j + 1) * TILE)
        acc = c_ref[:, at].astype(F32)
        if j:
            before = slice(0, j * TILE)
            acc = acc - (
                dot(wh[:, before], l_ref[at, before], NT)
                + dot(wl[:, before], l_ref[at, before], NT)
            )
        wh[:, at], wl[:, at] = split(dot3(acc, inv[j], NT))


def solve_constraint(l_ref, inv, wh, wl):
    ni = l_ref.shape[0]
    for j in reversed(range(ni // TILE)):
        at = slice(j * TILE, (j + 1) * TILE)
        acc = wh[:, at].astype(F32) + wl[:, at].astype(F32)
        if (j + 1) * TILE < ni:
            after = slice((j + 1) * TILE, ni)
            acc = acc + (dot(wh[:, after], l_ref[after, at]) + dot(wl[:, after], l_ref[after, at]))
        wh[:, at], wl[:, at] = split(-dot3(acc, inv[j]))


def tree(terms):
    terms = list(terms)
    while len(terms) > 1:
        terms = [sum(terms[i : i + 2][1:], terms[i]) for i in range(0, len(terms), 2)]
    return terms[0]


def tree(terms):
    terms = list(terms)
    while len(terms) > 1:
        terms = [sum(terms[i : i + 2][1:], terms[i]) for i in range(0, len(terms), 2)]
    return terms[0]


def solve_rows(small, rows):
    m = len(rows)
    s = [list(row) for row in small]
    rows = list(rows)
    left, out = {}, [None] * m
    for k in range(0, m, 2):
        after = range(k + 2, m)
        x, y, z = s[k][k], s[k][k + 1], s[k + 1][k + 1]
        scale = 1.0 / (x * z - y * y)
        ia, ib, ic = z * scale, -(y * scale), x * scale
        for j in after:
            u, v = s[k][j], s[k + 1][j]
            left[k, j] = (ia * u + ib * v, ib * u + ic * v)
        for j in after:
            a, b = left[k, j]
            for q in range(j, m):
                s[j][q] = s[j][q] - (a * s[k][q] + b * s[k + 1][q])
        for j in after:
            a, b = left[k, j]
            rows[j] = rows[j] - (a * rows[k] + b * rows[k + 1])
        out[k] = ia * rows[k] + ib * rows[k + 1]
        out[k + 1] = ib * rows[k] + ic * rows[k + 1]
    for k in reversed(range(0, m - 2, 2)):
        for t in range(2):
            out[k + t] = out[k + t] - tree(left[k, j][t] * out[j] for j in reversed(range(k + 2, m)))
    return out


def sweep(a, pivots=8):
    size = a.shape[0]
    lane = iota(a.shape, 1)
    row_at = iota(a.shape, 0)
    short = iota((pivots, size), 1)
    unit = iota((pivots, size), 0)
    span = range(pivots)
    for k in range(0, size, pivots):
        cols = [jnp.broadcast_to(a[:, k + i : k + i + 1], a.shape) for i in span]
        marked = jnp.where(short - k == unit, 1.0, 0.0)
        marked = jnp.where(short // pivots == k // pivots, marked, a[k : k + pivots, :])
        small = [[cols[max(i, j)][k + min(i, j) : k + min(i, j) + 1] for j in span] for i in span]
        fresh = solve_rows(small, [marked[i : i + 1] for i in span])
        a = jnp.where(lane // pivots == k // pivots, 0.0, a) - tree(cols[i] * fresh[i] for i in span)
        for i in span:
            a = jnp.where(row_at == k + i, fresh[i], a)
    return a


def turn(x, step):
    return jnp.concatenate([x[:, step:], x[:, :step]], axis=1)


def invert(ref, pin):
    step, n = pin.shape[0], ref.shape[0]
    count = n // step
    lane, unit = iota((step, n), 1), iota((step, n), 0)
    inside = lane < step
    eye = jnp.where(lane == unit, 1.0, 0.0)

    def panels():
        row = dot3(pin[...], jnp.where(inside, eye, ref[:step, :]))
        return row, [ref[i * step : (i + 1) * step, :] for i in range(1, count)]

    def finish(row, rest):
        for i, panel in enumerate(rest):
            panel = jnp.where(inside, 0.0, panel) - dot3(panel[:, :step], row)
            ref[i * step : (i + 1) * step, :] = turn(panel, step)
        ref[n - step :, :] = turn(row, step)

    def body(p, carry):
        row, rest = panels()
        ahead = rest[0][:, step : 2 * step] - dot3(rest[0][:, :step], row[:, step : 2 * step])
        pin[...] = sweep(ahead)
        finish(row, rest)
        return carry

    lax.fori_loop(0, count - 1, body, 0)
    finish(*panels())


STEP = 64


def stages_of(size):
    stages, stride = [], 1
    while stride < size:
        radix = 4 if stride * 4 <= size else 2
        stages.append((stride, radix))
        stride *= radix
    return stages


def at_device(sub, grp):
    return dict(device_id=(sub, grp), device_id_type=pl.DeviceIdType.MESH)


def pick(q, x):
    hi, lo = split(x)
    rest = (x - hi.astype(F32) - lo.astype(F32)).astype(BF16)
    return dot(q, hi) + dot(q, lo) + dot(q, rest)


def pick_columns(x, q):
    hi, lo = split(x)
    rest = (x - hi.astype(F32) - lo.astype(F32)).astype(BF16)
    return dot(hi, q, NT) + dot(lo, q, NT) + dot(rest, q, NT)


def reduction_kernel(
    l_hbm, c_hbm, rows_hbm, weights_hbm, bound_hbm, map_hbm, loads_hbm,
    red_ref, mass_ref, out_ref,
    l_ref, c_ref, weights_ref, bound, map_ref, loads_ref, stiff,
    inv, pickers, strips, wh, wl, move, came,
    work, lead, pin, z, step, near, acc, got, total, acc_last, got_last,
    local, send, recv, part_send, part_recv, fwd_send, fwd_recv,
    dir_send, dir_recv, sum_send, sum_recv, all_send, all_recv, last_send, last_recv,
):
    grp, sub = lax.axis_index("grp"), lax.axis_index("sub")
    members, size = lax.axis_size("grp"), lax.axis_size("sub")
    ahead, back = lax.rem(sub + 1, size), lax.rem(sub + size - 1, size)
    others = [lax.rem(grp + d, members) for d in range(1, members)]
    width = c_hbm.shape[0]
    half = map_ref.shape[1]
    n = loads_ref.shape[0]
    tiles = l_ref.shape[0] // TILE
    stages = stages_of(size)
    mine = pl.ds(pl.multiple_of(grp * width, width), width)
    share = half // members
    part = pl.ds(pl.multiple_of(grp * share, share), share)

    loads_in = []

    def load(src, dst):
        copy = pltpu.make_async_copy(src, dst, local.at[len(loads_in)])
        copy.start()
        loads_in.append(copy)

    spans = [slice(j * TILE, (j + 1) * TILE) for j in range(tiles)]
    for at in spans:
        load(l_hbm.at[at, at], l_ref.at[at, at])
    load(map_hbm, map_ref)
    load(c_hbm, c_ref.at[mine])
    load(rows_hbm, stiff.at[mine])
    load(bound_hbm, bound.at[grp])
    for j in range(1, tiles):
        before = slice(0, j * TILE)
        load(l_hbm.at[spans[j], before], l_ref.at[spans[j], before])
    load(weights_hbm, weights_ref)
    load(loads_hbm, loads_ref)

    def partner(stride, radix, d):
        digit = lax.rem(lax.div(sub, stride), radix)
        return sub + (lax.rem(digit + d, radix) - digit) * stride

    barrier = pltpu.get_barrier_semaphore()
    greeted = 0
    for other in others:
        pl.semaphore_signal(barrier, inc=1, **at_device(sub, other))
        greeted += 1
    for to in [ahead, back] + [partner(t, r, d) for t, r in stages for d in range(1, r)]:
        pl.semaphore_signal(barrier, inc=1, **at_device(to, grp))
        greeted += 1

    def remote(src, dst, send, recv, to_sub, to_grp):
        copy = pltpu.make_async_remote_copy(
            src_ref=src, dst_ref=dst, send_sem=send, recv_sem=recv, **at_device(to_sub, to_grp)
        )
        copy.start()
        return copy

    def spread(item, src, dst):
        return [
            remote(src, dst, send.at[item, d], recv.at[item, d], sub, other)
            for d, other in enumerate(others)
        ]

    def to_back(item, ref):
        return remote(ref.at[part], came.at[item, part], part_send.at[item], part_recv.at[item], back, grp)

    def forward(item):
        return [
            remote(
                came.at[item, part], came.at[item, part],
                fwd_send.at[item, d], fwd_recv.at[item, d], sub, other,
            )
            for d, other in enumerate(others)
        ]

    def finished(copies):
        for copy in copies:
            copy.wait()

    shared_in = []

    def exchange():
        finished(loads_in[tiles:])
        pl.semaphore_wait(barrier, greeted)
        shared_in.extend(spread(0, c_ref.at[mine], c_ref.at[mine]))
        shared_in.extend(spread(1, stiff.at[mine], stiff.at[mine]))
        shared_in.extend(spread(2, bound.at[grp], bound.at[grp]))

    pickers_of(pickers)
    finished(loads_in[:tiles])
    invert_diagonal(l_ref, inv, pickers, strips, exchange)
    finished(shared_in)

    q = jnp.where(iota((half, half), 0) == map_ref[...], 1.0, 0.0)
    qb = q.astype(BF16)
    c_ref[half:, :] = dot(qb, c_ref[half:, :]).astype(BF16)
    stiff[half:, :] = pick(qb, stiff[half:, :])
    stiff[half:, half:] = pick_columns(stiff[half:, half:], qb)
    solve_modes(l_ref, c_ref, inv, wh, wl)
    wo, ws = wh[:half, :], wh[half:, :]
    move[0] = stiff[half:, half:] - dot(ws, ws, NT)
    lead[0] = move[0, :STEP, :STEP]
    lead_move = remote(lead.at[0], lead.at[1], part_send.at[3], part_recv.at[3], back, grp)
    stiff_move = to_back(0, move.at[0])
    move[1] = stiff[half:, :half] - dot(ws, wo, NT)
    cross_move = to_back(1, move.at[1])
    work[...] = stiff[:half, :half] - dot(wo, wo, NT)

    solve_constraint(l_ref, inv, wh, wl)
    lead_move.wait()
    pin[...] = sweep(work[:STEP, :STEP] + lead[1])
    stiff_move.wait()
    forwards = forward(0)
    weights = weights_ref[...]
    eye = iota((half, half), 0) == iota((half, half), 1)
    pieces = jnp.concatenate([bound[i] for i in range(members)], axis=1)

    def mass_of(c, b):
        ch, cl = split(c.astype(F32) * weights)
        return dot(ch, c, NT) + dot(cl, c, NT) + jnp.where(eye, b, 0.0)

    placed = jnp.sum(q * pieces[:, half:], axis=1, keepdims=True)
    move[2] = mass_of(wh[half:, :], placed)
    mass_move = to_back(2, move.at[2])
    finished(forwards)
    reduced = work[...] + came[0]
    red_ref[...] = reduced
    work[...] = reduced
    invert(work, pin)

    z[...] = dot3(loads_ref[...], work[...])
    copies = [
        remote(z, near.at[0], dir_send.at[0], dir_recv.at[0], ahead, grp),
        remote(z, near.at[1], dir_send.at[1], dir_recv.at[1], back, grp),
    ]
    cross_move.wait()
    cross_forwards = forward(1)
    acc[0, :n, :n] = fdot(loads_ref[...], z[...], NT)
    acc[0, n:, n:] = jnp.zeros((n, n), F32)
    mass_ref[...] = mass_of(wh[:half, :], pieces[:, :half])
    mass_move.wait()
    mass_forwards = forward(2)
    finished(cross_forwards)
    finished(copies)
    pull = dot3(near[0], move[1]) + dot3(near[1], came[1], NT)
    step[...] = dot3(pull, work[...])
    copies = [remote(step, near.at[2], dir_send.at[2], dir_recv.at[2], ahead, grp)]
    acc[0, :n, n:] = fdot(z[...], pull, NT)
    acc[0, n:, :n] = fdot(pull, step[...], NT)

    rows = 2 * n // members
    chunk = pl.ds(pl.multiple_of(grp * rows, rows), rows)
    slots = [sum(r - 1 for _, r in stages[:i]) for i in range(len(stages))]

    def send_sums(i):
        stride, radix = stages[i]
        return [
            remote(
                acc.at[i, chunk], got.at[slots[i] + d - 1],
                sum_send.at[slots[i] + d - 1], sum_recv.at[slots[i] + d - 1],
                partner(stride, radix, d), grp,
            )
            for d in range(1, radix)
        ]

    def add_sums(i, copies):
        value = acc[i, chunk, :]
        for d, copy in enumerate(copies):
            copy.wait()
            value = value + got[slots[i] + d]
        acc[i + 1, chunk, :] = value

    def send_last(i):
        stride, radix = stages[i]
        return [
            remote(
                acc_last.at[i], got_last.at[slots[i] + d - 1],
                last_send.at[slots[i] + d - 1], last_recv.at[slots[i] + d - 1],
                partner(stride, radix, d), grp,
            )
            for d in range(1, radix)
        ]

    def add_last(i, copies):
        value = acc_last[i]
        for d, copy in enumerate(copies):
            copy.wait()
            value = value + got_last[slots[i] + d]
        acc_last[i + 1] = value

    final = len(stages)
    sums = send_sums(0)
    finished(mass_forwards)
    mass_ref[...] = mass_ref[...] + came[2]
    for i in range(1, final):
        add_sums(i - 1, sums)
        sums = send_sums(i)
    finished(copies)
    taken = dot3(near[2], move[1])
    turned = fdot(step[...], taken, NT) + fdot(taken, step[...], NT)
    acc_last[0] = jnp.concatenate([turned[: n // 2], turned[n // 2 :]], axis=1)
    lasts = send_last(0)
    add_sums(final - 1, sums)
    total[chunk, :] = acc[final, chunk, :]
    copies = [
        remote(acc.at[final, chunk], total.at[chunk], all_send.at[d], all_recv.at[d], sub, other)
        for d, other in enumerate(others)
    ]
    for i in range(1, final):
        add_last(i - 1, lasts)
        lasts = send_last(i)
    finished(copies)

    rho, side = total[:n, :n], total[:n, n:]
    bend = total[n:, :n]
    gamma, kappa = rho + side, side + bend
    gamma_inv = sweep(gamma)
    base = fdot(gamma_inv, rho)
    lift = fdot(gamma_inv, kappa)
    fixed = bend - fdot(kappa, lift)
    right = side - fdot(lift, rho, TN)
    add_last(final - 1, lasts)
    turned = jnp.concatenate([acc_last[final, :, :n], acc_last[final, :, n:]], axis=0)
    second = fdot(sweep(fixed + turned), right)
    out_ref[...] = fdot(base - fdot(lift, second), z[...], TN) + fdot(second, step[...], TN)


def hand_over(*refs):
    count = len(refs) // 2
    for src, dst in zip(refs[:count], refs[count:]):
        dst[...] = src[...]


def shards(
    interior_factor, coupling, boundary_stiffness, interior_mass, boundary_mass, dof_map, load_cases
):
    width, ni = coupling.shape[1:]
    nbound = boundary_stiffness.shape[2]
    half = nbound // 2
    n = load_cases.shape[1]
    size, members = lax.axis_size("sub"), lax.axis_size("grp")
    block = jax.ShapeDtypeStruct((half, half), F32)
    shapes = [block, block, jax.ShapeDtypeStruct((n, half), F32)]
    stages = stages_of(size)
    slots = sum(r - 1 for _, r in stages)
    peers = max(members - 1, 1)
    dma = pltpu.SemaphoreType.DMA
    vmem = pl.BlockSpec(memory_space=pltpu.VMEM)
    outs = pl.pallas_call(
        reduction_kernel,
        out_shape=shapes,
        in_specs=[pl.BlockSpec(memory_space=pltpu.HBM)] * 7,
        out_specs=[vmem] * 3,
        scratch_shapes=[
            pltpu.VMEM((ni, ni), BF16),
            pltpu.VMEM((nbound, ni), BF16),
            pltpu.VMEM((1, ni), F32),
            pltpu.VMEM((members, 1, width), F32),
            pltpu.VMEM((1, half), jnp.int32),
            pltpu.VMEM((n, half), F32),
            pltpu.VMEM((nbound, nbound), F32),
            pltpu.VMEM((ni // TILE, TILE, TILE), F32),
            pltpu.VMEM((BASE // 2, SMALL, 2 * SMALL), BF16),
            pltpu.VMEM((ni // SMALL * BASE, SMALL), F32),
            pltpu.VMEM((nbound, ni), BF16),
            pltpu.VMEM((nbound, ni), BF16),
            pltpu.VMEM((3, half, half), F32),
            pltpu.VMEM((3, half, half), F32),
            pltpu.VMEM((half, half), F32),
            pltpu.VMEM((2, STEP, STEP), F32),
            pltpu.VMEM((STEP, STEP), F32),
            pltpu.VMEM((n, half), F32),
            pltpu.VMEM((n, half), F32),
            pltpu.VMEM((3, n, half), F32),
            pltpu.VMEM((len(stages) + 1, 2 * n, 2 * n), F32),
            pltpu.VMEM((slots, 2 * n // members, 2 * n), F32),
            pltpu.VMEM((2 * n, 2 * n), F32),
            pltpu.VMEM((len(stages) + 1, n // 2, 2 * n), F32),
            pltpu.VMEM((slots, n // 2, 2 * n), F32),
            dma((2 * (ni // TILE) + 5,)),
            dma((3, peers)), dma((3, peers)), dma((4,)), dma((4,)), dma((3, peers)), dma((3, peers)),
            dma((3,)), dma((3,)), dma((slots,)), dma((slots,)), dma((peers,)), dma((peers,)),
            dma((slots,)), dma((slots,)),
        ],
        compiler_params=pltpu.CompilerParams(
            vmem_limit_bytes=VMEM_LIMIT, collective_id=0, has_side_effects=True
        ),
        name="reduction",
    )(
        interior_factor[0], coupling[0], boundary_stiffness[0], interior_mass,
        boundary_mass, dof_map, load_cases[0],
    )
    outs = pl.pallas_call(
        hand_over, out_shape=shapes, in_specs=[vmem] * 3, out_specs=[vmem] * 3, name="hand_over"
    )(*outs)
    return tuple(out[None] for out in outs)


def solution(mesh):
    return jax.shard_map(
        shards,
        mesh=mesh,
        in_specs=(
            P("sub", None, None),
            P("sub", "grp", None),
            P("sub", "grp", None),
            P("sub", None),
            P("sub", "grp"),
            P("sub", None),
            P("sub", None, None),
        ),
        out_specs=(P("sub", None, None), P("sub", None, None), P("sub", None, None)),
        check_vma=False,
    )
```

```python
import functools
import jax
import jax.numpy as jnp
from jax import lax
from jax.experimental import pallas as pl
from jax.experimental.pallas import tpu as pltpu
from jax.sharding import PartitionSpec as P

F32 = jnp.float32
BF16 = jnp.bfloat16
HIGH = lax.Precision.HIGHEST
SMALL = 128
BASE = 32
TILE = 256
VMEM_LIMIT = 56 * 2**20
NT = (((1,), (1,)), ((), ()))
NN = (((1,), (0,)), ((), ()))
TN = (((0,), (0,)), ((), ()))


def dot(a, b, dims=NN):
    return lax.dot_general(a, b, dims, preferred_element_type=F32)


def fdot(a, b, dims=NN):
    return lax.dot_general(a, b, dims, precision=HIGH, preferred_element_type=F32)


def split(x):
    hi = x.astype(BF16)
    return hi, (x - hi.astype(F32)).astype(BF16)


def dot3(a, b, dims=NN):
    ah, al = split(a)
    bh, bl = split(b)
    return dot(ah, bh, dims) + (dot(ah, bl, dims) + dot(al, bh, dims))


def iota(shape, dim):
    return lax.broadcasted_iota(jnp.int32, shape, dim)


def pickers_of(pickers):
    base = pickers.shape[0]
    rows = iota((SMALL, 2 * SMALL), 0)
    lane = iota((1, 2 * SMALL), 1)
    start = (lane & (SMALL - BASE)) + (lane >> SMALL.bit_length() - 1)
    for k in range(base):
        pickers[k] = jnp.where(rows == start + 2 * k, 1.0, 0.0).astype(BF16)


def invert_diagonal(l_ref, inv, pickers, strips):
    count = l_ref.shape[0] // SMALL
    rows = iota((SMALL, SMALL), 0)
    cols = iota((SMALL, SMALL), 1)
    bands = range(SMALL // BASE)

    def block(j):
        return l_ref[j * SMALL : (j + 1) * SMALL, j * SMALL : (j + 1) * SMALL]

    band = iota((BASE, SMALL), 1) >> BASE.bit_length() - 1
    for j in range(count):
        full = block(j).astype(F32)
        strips[j * BASE : (j + 1) * BASE, :] = sum(
            jnp.where(band == b, full[b * BASE : (b + 1) * BASE], 0.0) for b in bands
        )
    packed = jnp.concatenate(
        [strips[pl.ds(i, count, stride=BASE), :] for i in range(BASE)], axis=0
    ).astype(BF16)
    spread = [dot(packed[2 * k * count :], pickers[k]) for k in range(BASE // 2)]

    def entry(i, k):
        at = (i - (k & -2)) * count
        side = (k & 1) * SMALL
        return spread[k >> 1][at : at + count, side : side + SMALL]

    place = iota((count, SMALL), 1) & (BASE - 1)
    done = [jnp.where(place == i, 1.0, 0.0) for i in range(BASE)]
    scale = [1.0 / entry(i, i) for i in range(BASE)]
    for k in range(BASE):
        done[k] = done[k] * scale[k]
        for i in range(k + 1, BASE):
            done[i] = done[i] - entry(i, k) * done[k]
    for i in range(BASE):
        strips[pl.ds(i, count, stride=BASE), :] = done[i]

    xs = []
    for j in range(count):
        strip = strips[j * BASE : (j + 1) * BASE, :]
        xs.append(jnp.concatenate([jnp.where(band == b, strip, 0.0) for b in bands], axis=0))
    size = BASE
    while size < SMALL:
        same = (rows // (2 * size)) == (cols // (2 * size))
        mask = same & ((rows & size) > (cols & size))
        pairs = range(SMALL // (2 * size))
        for j in range(count):
            x = xs[j]
            parts = [x[p * size : (p + 1) * size] for p in range(2 * len(pairs))]
            low = jnp.concatenate(parts[1::2], axis=0)
            off = jnp.where(mask, block(j).astype(F32), 0.0).astype(BF16)
            lh, ll = split(low)
            xh, xl = split(x)
            mid = dot(jnp.concatenate([lh, ll], 1), jnp.concatenate([off, off], 0))
            mh, ml = split(mid)
            wide = dot(jnp.concatenate([mh, ml], 1), jnp.concatenate([xh, xh], 0)) + dot(mh, xl)
            low = low - wide
            for p in pairs:
                parts[2 * p + 1] = low[p * size : (p + 1) * size]
            xs[j] = jnp.concatenate(parts, axis=0)
        size *= 2

    for j in range(count // 2):
        upper, lower = xs[2 * j], xs[2 * j + 1]
        off = l_ref[(2 * j + 1) * SMALL : (2 * j + 2) * SMALL, 2 * j * SMALL : (2 * j + 1) * SMALL]
        lh, ll = split(lower)
        mid = dot(jnp.concatenate([lh, ll], 1), jnp.concatenate([off, off], 0))
        inv[j, :SMALL, :SMALL] = upper
        inv[j, :SMALL, SMALL:] = jnp.zeros((SMALL, SMALL), F32)
        inv[j, SMALL:, :SMALL] = -dot3(mid, upper)
        inv[j, SMALL:, SMALL:] = lower


def solve_modes(l_ref, c_ref, inv, wh, wl, done):
    for j in range(l_ref.shape[0] // TILE):
        at = slice(j * TILE, (j + 1) * TILE)
        acc = c_ref[:, at].astype(F32)
        if j:
            before = slice(0, j * TILE)
            acc = acc - (
                dot(wh[:, before], l_ref[at, before], NT)
                + dot(wl[:, before], l_ref[at, before], NT)
            )
        wh[:, at], wl[:, at] = split(dot3(acc, inv[j], NT))
        done(j)


def solve_constraint(l_ref, inv, wh, wl, done):
    ni = l_ref.shape[0]
    for j in reversed(range(ni // TILE)):
        at = slice(j * TILE, (j + 1) * TILE)
        acc = wh[:, at].astype(F32) + wl[:, at].astype(F32)
        if (j + 1) * TILE < ni:
            after = slice((j + 1) * TILE, ni)
            acc = acc + (dot(wh[:, after], l_ref[after, at]) + dot(wl[:, after], l_ref[after, at]))
        wh[:, at], wl[:, at] = split(-dot3(acc, inv[j]))
        done(j)


def tree(terms):
    terms = list(terms)
    while len(terms) > 1:
        terms = [sum(terms[i : i + 2][1:], terms[i]) for i in range(0, len(terms), 2)]
    return terms[0]


def tree(terms):
    terms = list(terms)
    while len(terms) > 1:
        terms = [sum(terms[i : i + 2][1:], terms[i]) for i in range(0, len(terms), 2)]
    return terms[0]


def solve_rows(small, rows):
    m = len(rows)
    s = [list(row) for row in small]
    rows = list(rows)
    left, out = {}, [None] * m
    for k in range(0, m, 2):
        after = range(k + 2, m)
        x, y, z = s[k][k], s[k][k + 1], s[k + 1][k + 1]
        scale = 1.0 / (x * z - y * y)
        ia, ib, ic = z * scale, -(y * scale), x * scale
        for j in after:
            u, v = s[k][j], s[k + 1][j]
            left[k, j] = (ia * u + ib * v, ib * u + ic * v)
        for j in after:
            a, b = left[k, j]
            for q in range(j, m):
                s[j][q] = s[j][q] - (a * s[k][q] + b * s[k + 1][q])
        for j in after:
            a, b = left[k, j]
            rows[j] = rows[j] - (a * rows[k] + b * rows[k + 1])
        out[k] = ia * rows[k] + ib * rows[k + 1]
        out[k + 1] = ib * rows[k] + ic * rows[k + 1]
    for k in reversed(range(0, m - 2, 2)):
        for t in range(2):
            out[k + t] = out[k + t] - tree(left[k, j][t] * out[j] for j in reversed(range(k + 2, m)))
    return out


def sweep(a, pivots=8):
    size = a.shape[0]
    lane = iota((pivots, size), 1)
    unit = iota((pivots, size), 0)
    span = range(pivots)
    blocks = [a[b : b + pivots, :] for b in range(0, size, pivots)]
    for p in range(len(blocks)):
        k = p * pivots
        inside = lane // pivots == p

        def spread(block):
            return [jnp.broadcast_to(block[:, k + i : k + i + 1], block.shape) for i in span]

        narrow = spread(blocks[p])
        small = [[narrow[max(i, j)][min(i, j) : min(i, j) + 1] for j in span] for i in span]
        marked = jnp.where(inside, jnp.where(lane - k == unit, 1.0, 0.0), blocks[p])
        fresh = solve_rows(small, [marked[i : i + 1] for i in span])
        wide = [jnp.broadcast_to(row, (pivots, size)) for row in fresh]
        for b in range(p + 1, p + len(blocks)):
            b = b % len(blocks)
            drop = tree(col * row for col, row in zip(spread(blocks[b]), wide))
            blocks[b] = jnp.where(inside, 0.0, blocks[b]) - drop
        blocks[p] = wide[0]
        for i in span[1:]:
            blocks[p] = jnp.where(unit == i, wide[i], blocks[p])
    return jnp.concatenate(blocks, axis=0)


def turn(x, step):
    return jnp.concatenate([x[:, step:], x[:, :step]], axis=1)


def invert(ref, pin, between):
    step, n = pin.shape[0], ref.shape[0]
    count = n // step
    lane, unit = iota((step, n), 1), iota((step, n), 0)
    inside = lane < step
    eye = jnp.where(lane == unit, 1.0, 0.0)

    def panels():
        row = dot3(pin[...], jnp.where(inside, eye, ref[:step, :]))
        return row, [ref[i * step : (i + 1) * step, :] for i in range(1, count)]

    def finish(row, rest):
        for i, panel in enumerate(rest):
            panel = jnp.where(inside, 0.0, panel) - dot3(panel[:, :step], row)
            ref[i * step : (i + 1) * step, :] = turn(panel, step)
        ref[n - step :, :] = turn(row, step)

    def body(p, carry):
        row, rest = panels()
        ahead = rest[0][:, step : 2 * step] - dot3(rest[0][:, :step], row[:, step : 2 * step])
        pin[...] = sweep(ahead)
        finish(row, rest)
        return carry

    lax.fori_loop(0, count - 1, body, 0)
    between()
    finish(*panels())


STEP = 64


def stages_of(size):
    stages, stride = [], 1
    while stride < size:
        radix = 4 if stride * 4 <= size else 2
        stages.append((stride, radix))
        stride *= radix
    return stages


def at_device(sub, grp):
    return dict(device_id=(sub, grp), device_id_type=pl.DeviceIdType.MESH)


def pick(q, x):
    hi, lo = split(x)
    rest = (x - hi.astype(F32) - lo.astype(F32)).astype(BF16)
    return dot(q, hi) + dot(q, lo) + dot(q, rest)


def pick_columns(x, q):
    hi, lo = split(x)
    rest = (x - hi.astype(F32) - lo.astype(F32)).astype(BF16)
    return dot(hi, q, NT) + dot(lo, q, NT) + dot(rest, q, NT)


def reduction_kernel(
    l_hbm, c_hbm, rows_hbm, weights_hbm, bound_hbm, map_hbm, loads_hbm,
    red_ref, mass_ref, out_ref,
    l_ref, c_ref, weights_ref, bound, map_ref, loads_ref, stiff,
    inv, pickers, strips, wh, wl, both, move, came,
    work, lead, pin, z, step, near, acc, got, total, acc_last, got_last,
    local, tile_send, tile_recv, send, recv, part_send, part_recv, fwd_send, fwd_recv,
    dir_send, dir_recv, sum_send, sum_recv, all_send, all_recv, last_send, last_recv,
):
    grp, sub = lax.axis_index("grp"), lax.axis_index("sub")
    members, size = lax.axis_size("grp"), lax.axis_size("sub")
    ahead, back = lax.rem(sub + 1, size), lax.rem(sub + size - 1, size)
    others = [lax.rem(grp + d, members) for d in range(1, members)]
    width = c_hbm.shape[0]
    half = map_ref.shape[1]
    n = loads_ref.shape[0]
    tiles = l_ref.shape[0] // TILE
    stages = stages_of(size)
    mine = pl.ds(pl.multiple_of(grp * width, width), width)
    share = half // members
    part = pl.ds(pl.multiple_of(grp * share, share), share)

    def partner(stride, radix, d):
        digit = lax.rem(lax.div(sub, stride), radix)
        return sub + (lax.rem(digit + d, radix) - digit) * stride

    barrier = pltpu.get_barrier_semaphore()
    greeted = 0
    for other in others:
        pl.semaphore_signal(barrier, inc=1, **at_device(sub, other))
        greeted += 1
    for to in [ahead, back] + [partner(t, r, d) for t, r in stages for d in range(1, r)]:
        pl.semaphore_signal(barrier, inc=1, **at_device(to, grp))
        greeted += 1

    loads_in = []

    def load(src, dst):
        copy = pltpu.make_async_copy(src, dst, local.at[len(loads_in)])
        copy.start()
        loads_in.append(copy)

    spans = [slice(j * TILE, (j + 1) * TILE) for j in range(tiles)]
    for at in spans:
        load(l_hbm.at[at, at], l_ref.at[at, at])
    load(map_hbm, map_ref)
    load(c_hbm, c_ref)
    load(rows_hbm, stiff.at[mine])
    load(bound_hbm, bound.at[grp])
    for j in range(1, tiles):
        before = slice(0, j * TILE)
        load(l_hbm.at[spans[j], before], l_ref.at[spans[j], before])
    load(weights_hbm, weights_ref)
    load(loads_hbm, loads_ref)

    def remote(src, dst, send, recv, to_sub, to_grp):
        copy = pltpu.make_async_remote_copy(
            src_ref=src, dst_ref=dst, send_sem=send, recv_sem=recv, **at_device(to_sub, to_grp)
        )
        copy.start()
        return copy

    def spread(item, src, dst):
        return [
            remote(src, dst, send.at[item, d], recv.at[item, d], sub, other)
            for d, other in enumerate(others)
        ]

    def to_back(item, ref):
        return remote(ref.at[part], came.at[item, part], part_send.at[item], part_recv.at[item], back, grp)

    def forward(item):
        return [
            remote(
                came.at[item, part], came.at[item, part],
                fwd_send.at[item, d], fwd_recv.at[item, d], sub, other,
            )
            for d, other in enumerate(others)
        ]

    def finished(copies):
        for copy in copies:
            copy.wait()

    pickers_of(pickers)
    finished(loads_in[:tiles])
    invert_diagonal(l_ref, inv, pickers, strips)
    finished(loads_in[tiles:])
    own_columns, shared_columns = pl.ds(0, half), pl.ds(half, half)
    first_in, later_in = [], []

    def spread_columns(item, columns):
        at = stiff.at[mine, columns]
        return spread(item, at, at)

    qb = jnp.where(iota((half, half), 0) == map_ref[...], 1.0, 0.0).astype(BF16)

    def share_tile(kind, j):
        both[kind, j, mine, :] = wh[:, spans[j]]
        at = both.at[kind, j, mine]
        return [
            remote(at, at, tile_send.at[kind, j, d], tile_recv.at[kind, j, d], sub, other)
            for d, other in enumerate(others)
        ]

    def place_tile(kind, j, copies):
        finished(copies)
        both[kind, j, half:, :] = dot(qb, both[kind, j, half:, :]).astype(BF16)

    def gram(j):
        shared = both[0, j, half:, :]
        return dot(shared, shared, NT)

    tile_copies = {}

    def mode_done(j):
        if j == 0:
            pl.semaphore_wait(barrier, greeted)
        tile_copies[j] = share_tile(0, j)
        if j == 0:
            first_in.extend(spread_columns(0, shared_columns))
        if j == tiles - 1:
            later_in.extend(spread_columns(1, own_columns))
            later_in.extend(spread(2, bound.at[grp], bound.at[grp]))
        if j == tiles - 2:
            finished(first_in)
            move[0] = pick_columns(pick(qb, stiff[half:, half:]), qb)
        if j:
            place_tile(0, j - 1, tile_copies[j - 1])

    solve_modes(l_ref, c_ref, inv, wh, wl, mode_done)
    partial = move[0] - sum(gram(j) for j in range(tiles - 1))
    place_tile(0, tiles - 1, tile_copies[tiles - 1])
    move[0] = partial - gram(tiles - 1)
    lead[0] = move[0, :STEP, :STEP]
    lead_move = remote(lead.at[0], lead.at[1], part_send.at[3], part_recv.at[3], back, grp)
    stiff_move = to_back(0, move.at[0])
    finished(later_in)
    move[1] = pick(qb, stiff[half:, :half]) - sum(dot(both[0, j, half:, :], both[0, j, :half, :], NT) for j in range(tiles))
    cross_move = to_back(1, move.at[1])
    work[...] = stiff[:half, :half] - sum(dot(both[0, j, :half, :], both[0, j, :half, :], NT) for j in range(tiles))

    def constraint_done(j):
        tile_copies[j] = share_tile(1, j)

    solve_constraint(l_ref, inv, wh, wl, constraint_done)
    lead_move.wait()
    pin[...] = sweep(work[:STEP, :STEP] + lead[1])
    stiff_move.wait()
    forwards = forward(0)
    eye = iota((half, half), 0) == iota((half, half), 1)
    pieces = jnp.concatenate([bound[i] for i in range(members)], axis=1)

    def mass_of(at, b):
        total = jnp.where(eye, b, 0.0)
        for j in range(tiles):
            c = both[1, j, at, :]
            ch, cl = split(c.astype(F32) * weights_ref[:, spans[j]])
            total = total + (dot(ch, c, NT) + dot(cl, c, NT))
        return total

    for j in range(tiles):
        place_tile(1, j, tile_copies[j])
    placed = jnp.sum(qb.astype(F32) * pieces[:, half:], axis=1, keepdims=True)
    move[2] = mass_of(slice(half, 2 * half), placed)
    mass_move = to_back(2, move.at[2])
    finished(forwards)
    reduced = work[...] + came[0]
    red_ref[...] = reduced
    work[...] = reduced
    late = []

    def pass_on():
        cross_move.wait()
        late.extend(forward(1))
        mass_move.wait()
        late.extend(forward(2))

    invert(work, pin, pass_on)

    rows = n // members
    chunk = pl.ds(pl.multiple_of(grp * rows, rows), rows)
    slots = [sum(r - 1 for _, r in stages[:i]) for i in range(len(stages))]
    final = len(stages)

    def send_sums(i):
        stride, radix = stages[i]
        return [
            remote(
                acc.at[i, chunk], got.at[slots[i] + d - 1],
                sum_send.at[slots[i] + d - 1], sum_recv.at[slots[i] + d - 1],
                partner(stride, radix, d), grp,
            )
            for d in range(1, radix)
        ]

    def add_sums(i, copies):
        value = acc[i, chunk, :]
        for d, copy in enumerate(copies):
            copy.wait()
            value = value + got[slots[i] + d]
        acc[i + 1, chunk, :] = value

    def folded(x):
        return jnp.concatenate([x[: n // 2], x[n // 2 :]], axis=1)

    def unfolded(x):
        return jnp.concatenate([x[:, :n], x[:, n:]], axis=0)

    def send_last(which, i):
        stride, radix = stages[i]
        return [
            remote(
                acc_last.at[which, i], got_last.at[which, slots[i] + d - 1],
                last_send.at[which, slots[i] + d - 1], last_recv.at[which, slots[i] + d - 1],
                partner(stride, radix, d), grp,
            )
            for d in range(1, radix)
        ]

    def add_last(which, i, copies):
        value = acc_last[which, i]
        for d, copy in enumerate(copies):
            copy.wait()
            value = value + got_last[which, slots[i] + d]
        acc_last[which, i + 1] = value

    z[...] = dot3(loads_ref[...], work[...])
    copies = [
        remote(z, near.at[0], dir_send.at[0], dir_recv.at[0], ahead, grp),
        remote(z, near.at[1], dir_send.at[1], dir_recv.at[1], back, grp),
    ]
    acc_last[0, 0] = folded(fdot(loads_ref[...], z[...], NT))
    firsts = send_last(0, 0)
    mass_ref[...] = mass_of(slice(0, half), pieces[:, :half])
    finished(late[:members - 1])
    finished(copies)
    pull = dot3(near[0], move[1]) + dot3(near[1], came[1], NT)
    step[...] = dot3(pull, work[...])
    copies = [remote(step, near.at[2], dir_send.at[2], dir_recv.at[2], ahead, grp)]
    acc[0, :, :n] = fdot(z[...], pull, NT)
    acc[0, :, n:] = fdot(pull, step[...], NT)

    sums = send_sums(0)
    finished(late[members - 1:])
    mass_ref[...] = mass_ref[...] + came[2]
    for i in range(1, final):
        add_last(0, i - 1, firsts)
        firsts = send_last(0, i)
        add_sums(i - 1, sums)
        sums = send_sums(i)
    finished(copies)
    taken = dot3(near[2], move[1])
    turned = fdot(step[...], taken, NT) + fdot(taken, step[...], NT)
    acc_last[1, 0] = folded(turned)
    lasts = send_last(1, 0)
    for i in range(1, final):
        add_last(1, i - 1, lasts)
        lasts = send_last(1, i)
    add_last(0, final - 1, firsts)
    add_sums(final - 1, sums)
    total[chunk, :] = acc[final, chunk, :]
    copies = [
        remote(acc.at[final, chunk], total.at[chunk], all_send.at[d], all_recv.at[d], sub, other)
        for d, other in enumerate(others)
    ]
    finished(copies)

    rho, side, bend = unfolded(acc_last[0, final]), total[:, :n], total[:, n:]
    gamma, kappa = rho + side, side + bend
    gamma_inv = sweep(gamma)
    base = fdot(gamma_inv, rho)
    lift = fdot(gamma_inv, kappa)
    fixed = bend - fdot(kappa, lift)
    right = side - fdot(lift, rho, TN)
    start = fdot(base, z[...], TN)
    other = step[...] - fdot(lift, z[...], TN)
    add_last(1, final - 1, lasts)
    second = fdot(sweep(fixed + unfolded(acc_last[1, final])), right)
    out_ref[...] = start + fdot(second, other, TN)


def hand_over(*refs):
    count = len(refs) // 2
    for src, dst in zip(refs[:count], refs[count:]):
        dst[...] = src[...]


def shards(
    interior_factor, coupling, boundary_stiffness, interior_mass, boundary_mass, dof_map, load_cases
):
    width, ni = coupling.shape[1:]
    nbound = boundary_stiffness.shape[2]
    half = nbound // 2
    n = load_cases.shape[1]
    size, members = lax.axis_size("sub"), lax.axis_size("grp")
    block = jax.ShapeDtypeStruct((half, half), F32)
    shapes = [block, block, jax.ShapeDtypeStruct((n, half), F32)]
    stages = stages_of(size)
    slots = sum(r - 1 for _, r in stages)
    peers = max(members - 1, 1)
    dma = pltpu.SemaphoreType.DMA
    vmem = pl.BlockSpec(memory_space=pltpu.VMEM)
    outs = pl.pallas_call(
        reduction_kernel,
        out_shape=shapes,
        in_specs=[pl.BlockSpec(memory_space=pltpu.HBM)] * 7,
        out_specs=[vmem] * 3,
        scratch_shapes=[
            pltpu.VMEM((ni, ni), BF16),
            pltpu.VMEM((width, ni), BF16),
            pltpu.VMEM((1, ni), F32),
            pltpu.VMEM((members, 1, width), F32),
            pltpu.VMEM((1, half), jnp.int32),
            pltpu.VMEM((n, half), F32),
            pltpu.VMEM((nbound, nbound), F32),
            pltpu.VMEM((ni // TILE, TILE, TILE), F32),
            pltpu.VMEM((BASE // 2, SMALL, 2 * SMALL), BF16),
            pltpu.VMEM((ni // SMALL * BASE, SMALL), F32),
            pltpu.VMEM((width, ni), BF16),
            pltpu.VMEM((width, ni), BF16),
            pltpu.VMEM((2, ni // TILE, nbound, TILE), BF16),
            pltpu.VMEM((3, half, half), F32),
            pltpu.VMEM((3, half, half), F32),
            pltpu.VMEM((half, half), F32),
            pltpu.VMEM((2, STEP, STEP), F32),
            pltpu.VMEM((STEP, STEP), F32),
            pltpu.VMEM((n, half), F32),
            pltpu.VMEM((n, half), F32),
            pltpu.VMEM((3, n, half), F32),
            pltpu.VMEM((len(stages) + 1, n, 2 * n), F32),
            pltpu.VMEM((slots, n // members, 2 * n), F32),
            pltpu.VMEM((n, 2 * n), F32),
            pltpu.VMEM((2, len(stages) + 1, n // 2, 2 * n), F32),
            pltpu.VMEM((2, slots, n // 2, 2 * n), F32),
            dma((2 * (ni // TILE) + 5,)),
            dma((2, ni // TILE, peers)), dma((2, ni // TILE, peers)), dma((3, peers)), dma((3, peers)),
            dma((4,)), dma((4,)), dma((3, peers)), dma((3, peers)),
            dma((3,)), dma((3,)), dma((slots,)), dma((slots,)), dma((peers,)), dma((peers,)),
            dma((2, slots)), dma((2, slots)),
        ],
        compiler_params=pltpu.CompilerParams(
            vmem_limit_bytes=VMEM_LIMIT, collective_id=0, has_side_effects=True
        ),
        name="reduction",
    )(
        interior_factor[0], coupling[0], boundary_stiffness[0], interior_mass,
        boundary_mass, dof_map, load_cases[0],
    )
    outs = pl.pallas_call(
        hand_over, out_shape=shapes, in_specs=[vmem] * 3, out_specs=[vmem] * 3, name="hand_over"
    )(*outs)
    return tuple(out[None] for out in outs)


def solution(mesh):
    return jax.shard_map(
        shards,
        mesh=mesh,
        in_specs=(
            P("sub", None, None),
            P("sub", "grp", None),
            P("sub", "grp", None),
            P("sub", None),
            P("sub", "grp"),
            P("sub", None),
            P("sub", None, None),
        ),
        out_specs=(P("sub", None, None), P("sub", None, None), P("sub", None, None)),
        check_vma=False,
    )
```

```python
import functools
import jax
import jax.numpy as jnp
from jax import lax
from jax.experimental import pallas as pl
from jax.experimental.pallas import tpu as pltpu
from jax.sharding import PartitionSpec as P

F32 = jnp.float32
BF16 = jnp.bfloat16
HIGH = lax.Precision.HIGHEST
SMALL = 128
BASE = 32
TILE = 256
VMEM_LIMIT = 56 * 2**20
NT = (((1,), (1,)), ((), ()))
NN = (((1,), (0,)), ((), ()))
TN = (((0,), (0,)), ((), ()))


def dot(a, b, dims=NN):
    return lax.dot_general(a, b, dims, preferred_element_type=F32)


def fdot(a, b, dims=NN):
    return lax.dot_general(a, b, dims, precision=HIGH, preferred_element_type=F32)


def split(x):
    hi = x.astype(BF16)
    return hi, (x - hi.astype(F32)).astype(BF16)


def dot3(a, b, dims=NN):
    ah, al = split(a)
    bh, bl = split(b)
    return dot(ah, bh, dims) + (dot(ah, bl, dims) + dot(al, bh, dims))


def iota(shape, dim):
    return lax.broadcasted_iota(jnp.int32, shape, dim)


def pickers_of(pickers):
    base = pickers.shape[0]
    rows = iota((SMALL, 2 * SMALL), 0)
    lane = iota((1, 2 * SMALL), 1)
    start = (lane & (SMALL - BASE)) + (lane >> SMALL.bit_length() - 1)
    for k in range(base):
        pickers[k] = jnp.where(rows == start + 2 * k, 1.0, 0.0).astype(BF16)


def invert_diagonal(l_ref, inv, pickers, strips):
    count = l_ref.shape[0] // SMALL
    rows = iota((SMALL, SMALL), 0)
    cols = iota((SMALL, SMALL), 1)
    bands = range(SMALL // BASE)

    def block(j):
        return l_ref[j * SMALL : (j + 1) * SMALL, j * SMALL : (j + 1) * SMALL]

    band = iota((BASE, SMALL), 1) >> BASE.bit_length() - 1
    for j in range(count):
        full = block(j).astype(F32)
        strips[j * BASE : (j + 1) * BASE, :] = sum(
            jnp.where(band == b, full[b * BASE : (b + 1) * BASE], 0.0) for b in bands
        )
    packed = jnp.concatenate(
        [strips[pl.ds(i, count, stride=BASE), :] for i in range(BASE)], axis=0
    ).astype(BF16)
    spread = [dot(packed[2 * k * count :], pickers[k]) for k in range(BASE // 2)]

    def entry(i, k):
        at = (i - (k & -2)) * count
        side = (k & 1) * SMALL
        return spread[k >> 1][at : at + count, side : side + SMALL]

    place = iota((count, SMALL), 1) & (BASE - 1)
    done = [jnp.where(place == i, 1.0, 0.0) for i in range(BASE)]
    scale = [1.0 / entry(i, i) for i in range(BASE)]
    for k in range(BASE):
        done[k] = done[k] * scale[k]
        for i in range(k + 1, BASE):
            done[i] = done[i] - entry(i, k) * done[k]
    for i in range(BASE):
        strips[pl.ds(i, count, stride=BASE), :] = done[i]

    xs = []
    for j in range(count):
        strip = strips[j * BASE : (j + 1) * BASE, :]
        xs.append(jnp.concatenate([jnp.where(band == b, strip, 0.0) for b in bands], axis=0))
    size = BASE
    while size < SMALL:
        same = (rows // (2 * size)) == (cols // (2 * size))
        mask = same & ((rows & size) > (cols & size))
        pairs = range(SMALL // (2 * size))
        for j in range(count):
            x = xs[j]
            parts = [x[p * size : (p + 1) * size] for p in range(2 * len(pairs))]
            low = jnp.concatenate(parts[1::2], axis=0)
            off = jnp.where(mask, block(j).astype(F32), 0.0).astype(BF16)
            lh, ll = split(low)
            xh, xl = split(x)
            mid = dot(jnp.concatenate([lh, ll], 1), jnp.concatenate([off, off], 0))
            mh, ml = split(mid)
            wide = dot(jnp.concatenate([mh, ml], 1), jnp.concatenate([xh, xh], 0)) + dot(mh, xl)
            low = low - wide
            for p in pairs:
                parts[2 * p + 1] = low[p * size : (p + 1) * size]
            xs[j] = jnp.concatenate(parts, axis=0)
        size *= 2

    for j in range(count // 2):
        upper, lower = xs[2 * j], xs[2 * j + 1]
        off = l_ref[(2 * j + 1) * SMALL : (2 * j + 2) * SMALL, 2 * j * SMALL : (2 * j + 1) * SMALL]
        lh, ll = split(lower)
        mid = dot(jnp.concatenate([lh, ll], 1), jnp.concatenate([off, off], 0))
        inv[j, :SMALL, :SMALL] = upper
        inv[j, :SMALL, SMALL:] = jnp.zeros((SMALL, SMALL), F32)
        inv[j, SMALL:, :SMALL] = -dot3(mid, upper)
        inv[j, SMALL:, SMALL:] = lower


def solve_modes(l_ref, c_ref, inv, wh, wl, done):
    for j in range(l_ref.shape[0] // TILE):
        at = slice(j * TILE, (j + 1) * TILE)
        acc = c_ref[:, at].astype(F32)
        if j:
            before = slice(0, j * TILE)
            acc = acc - (
                dot(wh[:, before], l_ref[at, before], NT)
                + dot(wl[:, before], l_ref[at, before], NT)
            )
        wh[:, at], wl[:, at] = split(dot3(acc, inv[j], NT))
        done(j)


def solve_constraint(l_ref, inv, wh, wl, done):
    ni = l_ref.shape[0]
    for j in reversed(range(ni // TILE)):
        at = slice(j * TILE, (j + 1) * TILE)
        acc = wh[:, at].astype(F32) + wl[:, at].astype(F32)
        if (j + 1) * TILE < ni:
            after = slice((j + 1) * TILE, ni)
            acc = acc + (dot(wh[:, after], l_ref[after, at]) + dot(wl[:, after], l_ref[after, at]))
        wh[:, at], wl[:, at] = split(-dot3(acc, inv[j]))
        done(j)


def tree(terms):
    terms = list(terms)
    while len(terms) > 1:
        terms = [sum(terms[i : i + 2][1:], terms[i]) for i in range(0, len(terms), 2)]
    return terms[0]


def tree(terms):
    terms = list(terms)
    while len(terms) > 1:
        terms = [sum(terms[i : i + 2][1:], terms[i]) for i in range(0, len(terms), 2)]
    return terms[0]


def solve_rows(small, rows):
    m = len(rows)
    s = [list(row) for row in small]
    rows = list(rows)
    left, out = {}, [None] * m
    for k in range(0, m, 2):
        after = range(k + 2, m)
        x, y, z = s[k][k], s[k][k + 1], s[k + 1][k + 1]
        scale = 1.0 / (x * z - y * y)
        ia, ib, ic = z * scale, -(y * scale), x * scale
        for j in after:
            u, v = s[k][j], s[k + 1][j]
            left[k, j] = (ia * u + ib * v, ib * u + ic * v)
        for j in after:
            a, b = left[k, j]
            for q in range(j, m):
                s[j][q] = s[j][q] - (a * s[k][q] + b * s[k + 1][q])
        for j in after:
            a, b = left[k, j]
            rows[j] = rows[j] - (a * rows[k] + b * rows[k + 1])
        out[k] = ia * rows[k] + ib * rows[k + 1]
        out[k + 1] = ib * rows[k] + ic * rows[k + 1]
    for k in reversed(range(0, m - 2, 2)):
        for t in range(2):
            out[k + t] = out[k + t] - tree(left[k, j][t] * out[j] for j in reversed(range(k + 2, m)))
    return out


def sweep(a, pivots=8):
    size = a.shape[0]
    lane = iota((pivots, size), 1)
    unit = iota((pivots, size), 0)
    span = range(pivots)
    blocks = [a[b : b + pivots, :] for b in range(0, size, pivots)]
    for p in range(len(blocks)):
        k = p * pivots
        inside = lane // pivots == p

        def spread(block):
            return [jnp.broadcast_to(block[:, k + i : k + i + 1], block.shape) for i in span]

        narrow = spread(blocks[p])
        small = [[narrow[max(i, j)][min(i, j) : min(i, j) + 1] for j in span] for i in span]
        marked = jnp.where(inside, jnp.where(lane - k == unit, 1.0, 0.0), blocks[p])
        fresh = solve_rows(small, [marked[i : i + 1] for i in span])
        wide = [jnp.broadcast_to(row, (pivots, size)) for row in fresh]
        for b in range(p + 1, p + len(blocks)):
            b = b % len(blocks)
            drop = tree(col * row for col, row in zip(spread(blocks[b]), wide))
            blocks[b] = jnp.where(inside, 0.0, blocks[b]) - drop
        blocks[p] = wide[0]
        for i in span[1:]:
            blocks[p] = jnp.where(unit == i, wide[i], blocks[p])
    return jnp.concatenate(blocks, axis=0)


def turn(x, step):
    return jnp.concatenate([x[:, step:], x[:, :step]], axis=1)


def invert(ref, pin, between):
    step, n = pin.shape[0], ref.shape[0]
    count = n // step
    lane, unit = iota((step, n), 1), iota((step, n), 0)
    inside = lane < step
    eye = jnp.where(lane == unit, 1.0, 0.0)

    def panels():
        row = dot3(pin[...], jnp.where(inside, eye, ref[:step, :]))
        return row, [ref[i * step : (i + 1) * step, :] for i in range(1, count)]

    def finish(row, rest):
        for i, panel in enumerate(rest):
            panel = jnp.where(inside, 0.0, panel) - dot3(panel[:, :step], row)
            ref[i * step : (i + 1) * step, :] = turn(panel, step)
        ref[n - step :, :] = turn(row, step)

    def body(p, carry):
        row, rest = panels()
        ahead = rest[0][:, step : 2 * step] - dot3(rest[0][:, :step], row[:, step : 2 * step])
        pin[...] = sweep(ahead)
        finish(row, rest)
        return carry

    lax.fori_loop(0, count - 1, body, 0)
    between()
    finish(*panels())


STEP = 128


def stages_of(size):
    stages, stride = [], 1
    while stride < size:
        radix = 4 if stride * 4 <= size else 2
        stages.append((stride, radix))
        stride *= radix
    return stages


def at_device(sub, grp):
    return dict(device_id=(sub, grp), device_id_type=pl.DeviceIdType.MESH)


def pick(q, x):
    hi, lo = split(x)
    rest = (x - hi.astype(F32) - lo.astype(F32)).astype(BF16)
    return dot(q, hi) + dot(q, lo) + dot(q, rest)


def pick_columns(x, q):
    hi, lo = split(x)
    rest = (x - hi.astype(F32) - lo.astype(F32)).astype(BF16)
    return dot(hi, q, NT) + dot(lo, q, NT) + dot(rest, q, NT)


def reduction_kernel(
    l_hbm, c_hbm, rows_hbm, weights_hbm, bound_hbm, map_hbm, loads_hbm,
    red_hbm, mass_hbm, out_ref,
    red_ref, mass_ref,
    l_ref, c_ref, weights_ref, bound, map_ref, loads_ref, stiff,
    inv, pickers, strips, wh, wl, both, move, came,
    work, lead, pin, z, step, near, acc, got, total, acc_last, got_last,
    local, out_sem, tile_send, tile_recv, send, recv, part_send, part_recv, fwd_send, fwd_recv,
    dir_send, dir_recv, sum_send, sum_recv, all_send, all_recv, last_send, last_recv,
):
    grp, sub = lax.axis_index("grp"), lax.axis_index("sub")
    members, size = lax.axis_size("grp"), lax.axis_size("sub")
    ahead, back = lax.rem(sub + 1, size), lax.rem(sub + size - 1, size)
    others = [lax.rem(grp + d, members) for d in range(1, members)]
    width = c_hbm.shape[0]
    half = map_ref.shape[1]
    n = loads_ref.shape[0]
    tiles = l_ref.shape[0] // TILE
    stages = stages_of(size)
    mine = pl.ds(pl.multiple_of(grp * width, width), width)
    share = half // members
    part = pl.ds(pl.multiple_of(grp * share, share), share)

    def partner(stride, radix, d):
        digit = lax.rem(lax.div(sub, stride), radix)
        return sub + (lax.rem(digit + d, radix) - digit) * stride

    barrier = pltpu.get_barrier_semaphore()
    greeted = 0
    for other in others:
        pl.semaphore_signal(barrier, inc=1, **at_device(sub, other))
        greeted += 1
    for to in [ahead, back] + [partner(t, r, d) for t, r in stages for d in range(1, r)]:
        pl.semaphore_signal(barrier, inc=1, **at_device(to, grp))
        greeted += 1

    loads_in = []

    def load(src, dst):
        copy = pltpu.make_async_copy(src, dst, local.at[len(loads_in)])
        copy.start()
        loads_in.append(copy)

    spans = [slice(j * TILE, (j + 1) * TILE) for j in range(tiles)]
    for at in spans:
        load(l_hbm.at[at, at], l_ref.at[at, at])
    load(map_hbm, map_ref)
    load(c_hbm, c_ref)
    load(rows_hbm, stiff.at[mine])
    load(bound_hbm, bound.at[grp])
    for j in range(1, tiles):
        before = slice(0, j * TILE)
        load(l_hbm.at[spans[j], before], l_ref.at[spans[j], before])
    load(weights_hbm, weights_ref)
    load(loads_hbm, loads_ref)

    def remote(src, dst, send, recv, to_sub, to_grp):
        copy = pltpu.make_async_remote_copy(
            src_ref=src, dst_ref=dst, send_sem=send, recv_sem=recv, **at_device(to_sub, to_grp)
        )
        copy.start()
        return copy

    def spread(item, src, dst):
        return [
            remote(src, dst, send.at[item, d], recv.at[item, d], sub, other)
            for d, other in enumerate(others)
        ]

    def to_back(item, ref):
        return remote(ref.at[part], came.at[item, part], part_send.at[item], part_recv.at[item], back, grp)

    def forward(item):
        return [
            remote(
                came.at[item, part], came.at[item, part],
                fwd_send.at[item, d], fwd_recv.at[item, d], sub, other,
            )
            for d, other in enumerate(others)
        ]

    def finished(copies):
        for copy in copies:
            copy.wait()

    pickers_of(pickers)
    finished(loads_in[:tiles])
    invert_diagonal(l_ref, inv, pickers, strips)
    finished(loads_in[tiles:])
    own_columns, shared_columns = pl.ds(0, half), pl.ds(half, half)
    first_in, later_in = [], []

    def spread_columns(item, columns):
        at = stiff.at[mine, columns]
        return spread(item, at, at)

    qb = jnp.where(iota((half, half), 0) == map_ref[...], 1.0, 0.0).astype(BF16)

    def share_tile(kind, j):
        both[kind, j, mine, :] = wh[:, spans[j]]
        at = both.at[kind, j, mine]
        return [
            remote(at, at, tile_send.at[kind, j, d], tile_recv.at[kind, j, d], sub, other)
            for d, other in enumerate(others)
        ]

    def place_tile(kind, j, copies):
        finished(copies)
        both[kind, j, half:, :] = dot(qb, both[kind, j, half:, :]).astype(BF16)

    def gram(j):
        shared = both[0, j, half:, :]
        return dot(shared, shared, NT)

    tile_copies = {}

    def mode_done(j):
        if j == 0:
            pl.semaphore_wait(barrier, greeted)
        tile_copies[j] = share_tile(0, j)
        if j == 0:
            first_in.extend(spread_columns(0, shared_columns))
        if j == tiles - 1:
            later_in.extend(spread_columns(1, own_columns))
            later_in.extend(spread(2, bound.at[grp], bound.at[grp]))
        if j == tiles - 2:
            finished(first_in)
            move[0] = pick_columns(pick(qb, stiff[half:, half:]), qb)
        if j:
            place_tile(0, j - 1, tile_copies[j - 1])

    solve_modes(l_ref, c_ref, inv, wh, wl, mode_done)
    partial = move[0] - sum(gram(j) for j in range(tiles - 1))
    place_tile(0, tiles - 1, tile_copies[tiles - 1])
    move[0] = partial - gram(tiles - 1)
    lead[0] = move[0, :STEP, :STEP]
    lead_move = remote(lead.at[0], lead.at[1], part_send.at[3], part_recv.at[3], back, grp)
    stiff_move = to_back(0, move.at[0])
    finished(later_in)
    move[1] = pick(qb, stiff[half:, :half]) - sum(dot(both[0, j, half:, :], both[0, j, :half, :], NT) for j in range(tiles))
    cross_move = to_back(1, move.at[1])
    work[...] = stiff[:half, :half] - sum(dot(both[0, j, :half, :], both[0, j, :half, :], NT) for j in range(tiles))

    def constraint_done(j):
        tile_copies[j] = share_tile(1, j)

    solve_constraint(l_ref, inv, wh, wl, constraint_done)
    lead_move.wait()
    pin[...] = sweep(work[:STEP, :STEP] + lead[1])
    stiff_move.wait()
    forwards = forward(0)
    eye = iota((half, half), 0) == iota((half, half), 1)
    pieces = jnp.concatenate([bound[i] for i in range(members)], axis=1)

    def mass_of(at, b):
        total = jnp.where(eye, b, 0.0)
        for j in range(tiles):
            c = both[1, j, at, :]
            ch, cl = split(c.astype(F32) * weights_ref[:, spans[j]])
            total = total + (dot(ch, c, NT) + dot(cl, c, NT))
        return total

    for j in range(tiles):
        place_tile(1, j, tile_copies[j])
    placed = jnp.sum(qb.astype(F32) * pieces[:, half:], axis=1, keepdims=True)
    move[2] = mass_of(slice(half, 2 * half), placed)
    mass_move = to_back(2, move.at[2])
    finished(forwards)
    reduced = work[...] + came[0]
    red_ref[...] = reduced
    red_out = pltpu.make_async_copy(red_ref, red_hbm, out_sem.at[0])
    red_out.start()
    work[...] = reduced
    late = []

    def pass_on():
        cross_move.wait()
        late.extend(forward(1))
        mass_move.wait()
        late.extend(forward(2))

    invert(work, pin, pass_on)

    rows = n // members
    chunk = pl.ds(pl.multiple_of(grp * rows, rows), rows)
    slots = [sum(r - 1 for _, r in stages[:i]) for i in range(len(stages))]
    final = len(stages)

    def send_sums(i):
        stride, radix = stages[i]
        return [
            remote(
                acc.at[i, chunk], got.at[slots[i] + d - 1],
                sum_send.at[slots[i] + d - 1], sum_recv.at[slots[i] + d - 1],
                partner(stride, radix, d), grp,
            )
            for d in range(1, radix)
        ]

    def add_sums(i, copies):
        value = acc[i, chunk, :]
        for d, copy in enumerate(copies):
            copy.wait()
            value = value + got[slots[i] + d]
        acc[i + 1, chunk, :] = value

    def folded(x):
        return jnp.concatenate([x[: n // 2], x[n // 2 :]], axis=1)

    def unfolded(x):
        return jnp.concatenate([x[:, :n], x[:, n:]], axis=0)

    def send_last(which, i):
        stride, radix = stages[i]
        return [
            remote(
                acc_last.at[which, i], got_last.at[which, slots[i] + d - 1],
                last_send.at[which, slots[i] + d - 1], last_recv.at[which, slots[i] + d - 1],
                partner(stride, radix, d), grp,
            )
            for d in range(1, radix)
        ]

    def add_last(which, i, copies):
        value = acc_last[which, i]
        for d, copy in enumerate(copies):
            copy.wait()
            value = value + got_last[which, slots[i] + d]
        acc_last[which, i + 1] = value

    z[...] = dot3(loads_ref[...], work[...])
    copies = [
        remote(z, near.at[0], dir_send.at[0], dir_recv.at[0], ahead, grp),
        remote(z, near.at[1], dir_send.at[1], dir_recv.at[1], back, grp),
    ]
    acc_last[0, 0] = folded(fdot(loads_ref[...], z[...], NT))
    firsts = send_last(0, 0)
    mass_ref[...] = mass_of(slice(0, half), pieces[:, :half])
    finished(late[:members - 1])
    finished(copies)
    pull = dot3(near[0], move[1]) + dot3(near[1], came[1], NT)
    step[...] = dot3(pull, work[...])
    copies = [remote(step, near.at[2], dir_send.at[2], dir_recv.at[2], ahead, grp)]
    acc[0, :, :n] = fdot(z[...], pull, NT)
    acc[0, :, n:] = fdot(pull, step[...], NT)

    sums = send_sums(0)
    finished(late[members - 1:])
    mass_ref[...] = mass_ref[...] + came[2]
    mass_out = pltpu.make_async_copy(mass_ref, mass_hbm, out_sem.at[1])
    mass_out.start()
    for i in range(1, final):
        add_last(0, i - 1, firsts)
        firsts = send_last(0, i)
        add_sums(i - 1, sums)
        sums = send_sums(i)
    finished(copies)
    taken = dot3(near[2], move[1])
    turned = fdot(step[...], taken, NT) + fdot(taken, step[...], NT)
    acc_last[1, 0] = folded(turned)
    lasts = send_last(1, 0)
    for i in range(1, final):
        add_last(1, i - 1, lasts)
        lasts = send_last(1, i)
    add_last(0, final - 1, firsts)
    add_sums(final - 1, sums)
    total[chunk, :] = acc[final, chunk, :]
    copies = [
        remote(acc.at[final, chunk], total.at[chunk], all_send.at[d], all_recv.at[d], sub, other)
        for d, other in enumerate(others)
    ]
    finished(copies)

    rho, side, bend = unfolded(acc_last[0, final]), total[:, :n], total[:, n:]
    gamma, kappa = rho + side, side + bend
    gamma_inv = sweep(gamma)
    base = fdot(gamma_inv, rho)
    lift = fdot(gamma_inv, kappa)
    fixed = bend - fdot(kappa, lift)
    right = side - fdot(lift, rho, TN)
    start = fdot(base, z[...], TN)
    other = step[...] - fdot(lift, z[...], TN)
    add_last(1, final - 1, lasts)
    second = fdot(sweep(fixed + unfolded(acc_last[1, final])), right)
    out_ref[...] = start + fdot(second, other, TN)
    red_out.wait()
    mass_out.wait()


def hand_over(*refs):
    count = len(refs) // 2
    for src, dst in zip(refs[:count], refs[count:]):
        dst[...] = src[...]


def shards(
    interior_factor, coupling, boundary_stiffness, interior_mass, boundary_mass, dof_map, load_cases
):
    width, ni = coupling.shape[1:]
    nbound = boundary_stiffness.shape[2]
    half = nbound // 2
    n = load_cases.shape[1]
    size, members = lax.axis_size("sub"), lax.axis_size("grp")
    block = jax.ShapeDtypeStruct((half, half), F32)
    shapes = [block, block, jax.ShapeDtypeStruct((n, half), F32)]
    stages = stages_of(size)
    slots = sum(r - 1 for _, r in stages)
    peers = max(members - 1, 1)
    dma = pltpu.SemaphoreType.DMA
    vmem = pl.BlockSpec(memory_space=pltpu.VMEM)
    outs = pl.pallas_call(
        reduction_kernel,
        out_shape=shapes,
        in_specs=[pl.BlockSpec(memory_space=pltpu.HBM)] * 7,
        out_specs=[pl.BlockSpec(memory_space=pltpu.HBM)] * 2 + [vmem],
        scratch_shapes=[
            pltpu.VMEM((half, half), F32),
            pltpu.VMEM((half, half), F32),
            pltpu.VMEM((ni, ni), BF16),
            pltpu.VMEM((width, ni), BF16),
            pltpu.VMEM((1, ni), F32),
            pltpu.VMEM((members, 1, width), F32),
            pltpu.VMEM((1, half), jnp.int32),
            pltpu.VMEM((n, half), F32),
            pltpu.VMEM((nbound, nbound), F32),
            pltpu.VMEM((ni // TILE, TILE, TILE), F32),
            pltpu.VMEM((BASE // 2, SMALL, 2 * SMALL), BF16),
            pltpu.VMEM((ni // SMALL * BASE, SMALL), F32),
            pltpu.VMEM((width, ni), BF16),
            pltpu.VMEM((width, ni), BF16),
            pltpu.VMEM((2, ni // TILE, nbound, TILE), BF16),
            pltpu.VMEM((3, half, half), F32),
            pltpu.VMEM((3, half, half), F32),
            pltpu.VMEM((half, half), F32),
            pltpu.VMEM((2, STEP, STEP), F32),
            pltpu.VMEM((STEP, STEP), F32),
            pltpu.VMEM((n, half), F32),
            pltpu.VMEM((n, half), F32),
            pltpu.VMEM((3, n, half), F32),
            pltpu.VMEM((len(stages) + 1, n, 2 * n), F32),
            pltpu.VMEM((slots, n // members, 2 * n), F32),
            pltpu.VMEM((n, 2 * n), F32),
            pltpu.VMEM((2, len(stages) + 1, n // 2, 2 * n), F32),
            pltpu.VMEM((2, slots, n // 2, 2 * n), F32),
            dma((2 * (ni // TILE) + 5,)),
            dma((2,)),
            dma((2, ni // TILE, peers)), dma((2, ni // TILE, peers)), dma((3, peers)), dma((3, peers)),
            dma((4,)), dma((4,)), dma((3, peers)), dma((3, peers)),
            dma((3,)), dma((3,)), dma((slots,)), dma((slots,)), dma((peers,)), dma((peers,)),
            dma((2, slots)), dma((2, slots)),
        ],
        compiler_params=pltpu.CompilerParams(
            vmem_limit_bytes=VMEM_LIMIT, collective_id=0, has_side_effects=True
        ),
        name="reduction",
    )(
        interior_factor[0], coupling[0], boundary_stiffness[0], interior_mass,
        boundary_mass, dof_map, load_cases[0],
    )
    outs = pl.pallas_call(
        hand_over, out_shape=shapes, in_specs=[vmem] * 3, out_specs=[vmem] * 3, name="hand_over"
    )(*outs)
    return tuple(out[None] for out in outs)


def solution(mesh):
    return jax.shard_map(
        shards,
        mesh=mesh,
        in_specs=(
            P("sub", None, None),
            P("sub", "grp", None),
            P("sub", "grp", None),
            P("sub", None),
            P("sub", "grp"),
            P("sub", None),
            P("sub", None, None),
        ),
        out_specs=(P("sub", None, None), P("sub", None, None), P("sub", None, None)),
        check_vma=False,
    )
```
